32 devices in a mesh: dp: 8 (over z, core), ctx: 4 (over y, x).
Axes of the slice: x: 2, y: 2, z: 4, core: 2. Of those that a mesh axis runs over, the one named last changes fastest.
Arguments:
- layer_input: bfloat16 [8, 640, 4096], P('dp', 'ctx'), may hold values from -6 to 6
- queries: bfloat16 [8, 640, 2048], P('dp', 'ctx'), may hold values from -6 to 6, as said below
- key_rows: bfloat16 [8, 640, 2048], P('dp', 'ctx'), may hold values from -6 to 6, as said below
- value_rows: bfloat16 [8, 640, 2048], P('dp', 'ctx'), may hold values from -6 to 6
- attn_out: bfloat16 [8, 640, 2048], P('dp', 'ctx'), may hold values from -3 to 3
- out_grad: bfloat16 [8, 640, 2048], P('dp', 'ctx'), may hold values from -0.15625 to 0.15625
- layer_grad: bfloat16 [8, 640, 4096], P('dp', 'ctx'), may hold values from -0.078125 to 0.078125
- logsum: float32 [8, 16, 640], P('dp'), may hold values from -12 to 16, as said below
- projector: bfloat16 [4096, 512], replicated, may hold values from -0.09375 to 0.09375
Outputs:
- weight_grads: float32 [4, 512, 2048], P(None, ('dp', 'ctx'))
The draws below stay inside these ranges and needn't reach their ends.
Inputs may be any that keep to these rules, and one draw needn't show every extreme that they name: `queries`: drawn together with key_rows and logsum. `key_rows`: drawn together with queries and logsum. logsum[s, h, t] is the logarithm of the sum over u <= t of exp(scores[s, h, t, u]), scores as in the reference program, from the bfloat16 queries and key_rows.
All inputs are finite; a program needn't handle non-finite values.
Results may differ from the reference program's by a relative error of at most 0.0033.
Values may be sent and summed in bfloat16 or wider, within the bound.
A program may use at most 320 MiB of HBM per device.

```python
import math
import jax
import jax.numpy as jnp
from jax import lax

D = 4096
HEADS = 16
HEAD_DIM = 128
RANK = 512
TOKENS = 640
SEQS = 8


def joint_draw(key):
    query_key = jax.random.fold_in(key, 101)
    other_key = jax.random.fold_in(key, 202)
    shape = (SEQS, TOKENS, HEADS * HEAD_DIM)
    first = jnp.clip(jax.random.normal(query_key, shape, jnp.float32), -6.0, 6.0)
    second = jnp.clip(jax.random.normal(other_key, shape, jnp.float32), -6.0, 6.0)
    return (first.astype(jnp.bfloat16), second.astype(jnp.bfloat16))


def draw_queries(key, part):
    return joint_draw(key)[0]


def draw_key_rows(key, part):
    return joint_draw(key)[1]


def draw_logsum(key, part):
    first, second = joint_draw(key)
    scaling = 1.0 / math.sqrt(HEAD_DIM)

    def one_sequence(members):
        query_seq, key_seq = members
        query3 = query_seq.astype(jnp.float32).reshape(TOKENS, HEADS, HEAD_DIM)
        key3 = key_seq.astype(jnp.float32).reshape(TOKENS, HEADS, HEAD_DIM)
        scores = jnp.einsum('thd,uhd->htu', query3, key3, precision=lax.Precision.HIGHEST) * scaling
        positions = lax.iota(jnp.int32, TOKENS)
        causal = positions[:, None] >= positions[None, :]
        masked = jnp.where(causal[None], scores, jnp.float32(-1e+30))
        return jax.scipy.special.logsumexp(masked, axis=-1)
    return lax.map(one_sequence, (first, second))


def levels(stream_key, dims, cuts, least, top_value):
    def one(dim, blocks):
        draws = jax.random.uniform(jax.random.fold_in(jax.random.fold_in(stream_key, 6), dim), (blocks,), jnp.float32, least / len(cuts), top_value / len(cuts))
        return jnp.repeat(jnp.exp(draws), dims[dim] // blocks).reshape((-1,) + (1,) * (len(dims) - dim - 1))

    gain = one(*cuts[0])
    for cut in cuts[1:]:
        gain = gain * one(*cut)
    return gain


def normal_values(own_key, extent, scale, bound, shards=(), dtype=jnp.bfloat16):
    factor_of = levels(own_key, extent, shards, -0.22, 0.18) if shards else 1.0
    entries = jax.random.normal(own_key, extent, jnp.float32) * scale * factor_of
    return jnp.minimum(jnp.maximum(entries, -bound), bound).astype(dtype)


def setup_inputs(seed: int = 0) -> dict:
    keys = jax.random.split(jax.random.key(seed), 10)
    return {
        "layer_input": normal_values(keys[0], (SEQS, TOKENS, D), 1.0, 6.0, ((0, 8), (1, 4))),
        "queries": draw_queries(jax.random.fold_in(keys[9], 71), 0),
        "key_rows": draw_key_rows(jax.random.fold_in(keys[9], 71), 0),
        "value_rows": normal_values(keys[3], (SEQS, TOKENS, HEADS * HEAD_DIM), 1.0, 6.0, ((0, 8), (1, 4))),
        "attn_out": normal_values(keys[4], (SEQS, TOKENS, HEADS * HEAD_DIM), 0.5, 3.0, ((0, 8), (1, 4))),
        "out_grad": normal_values(keys[5], (SEQS, TOKENS, HEADS * HEAD_DIM), (2.0 / (SEQS * TOKENS) ** 0.5), 0.15625, ((0, 8), (1, 4))),
        "layer_grad": normal_values(keys[6], (SEQS, TOKENS, D), (1.0 / (SEQS * TOKENS) ** 0.5), 0.078125, ((0, 8), (1, 4))),
        "logsum": draw_logsum(jax.random.fold_in(keys[9], 71), 0),
        "projector": normal_values(keys[8], (D, RANK), D ** -0.5, 0.09375),
    }


def reference(layer_input, queries, key_rows, value_rows, attn_out, out_grad, layer_grad, logsum, projector):
    scaling = 1.0 / math.sqrt(HEAD_DIM)
    feature_width = HEADS * HEAD_DIM
    highest = lax.Precision.HIGHEST

    def one_sequence(totals, members):
        input_seq, query_seq, key_seq, value_seq, out_seq, grad_seq, layer_seq, logsum_seq = members
        reduced_in = jnp.dot(input_seq, projector, preferred_element_type=jnp.float32).astype(jnp.bfloat16)
        reduced_grad = jnp.dot(layer_seq, projector, preferred_element_type=jnp.float32).astype(jnp.bfloat16)
        query3 = query_seq.astype(jnp.float32).reshape(TOKENS, HEADS, HEAD_DIM)
        key3 = key_seq.astype(jnp.float32).reshape(TOKENS, HEADS, HEAD_DIM)
        value3 = value_seq.astype(jnp.float32).reshape(TOKENS, HEADS, HEAD_DIM)
        grad3 = grad_seq.astype(jnp.float32).reshape(TOKENS, HEADS, HEAD_DIM)
        out3 = out_seq.astype(jnp.float32).reshape(TOKENS, HEADS, HEAD_DIM)
        scores = jnp.einsum('thd,uhd->htu', query3, key3, precision=highest) * scaling
        positions = lax.iota(jnp.int32, TOKENS)
        causal = positions[:, None] >= positions[None, :]
        prob = jnp.where(causal[None], jnp.exp(scores - logsum_seq[:, :, None]), jnp.float32(0.0))
        deltas = lax.optimization_barrier(jnp.sum(grad3 * out3, axis=-1)).T
        dprob = jnp.einsum('thd,uhd->htu', grad3, value3, precision=highest)
        dscore = prob * (dprob - deltas[:, :, None]) * scaling
        score_low = lax.optimization_barrier(dscore.astype(jnp.bfloat16)).astype(jnp.float32)
        prob_low = lax.optimization_barrier(prob.astype(jnp.bfloat16)).astype(jnp.float32)
        dquery = jnp.einsum('htu,uhd->thd', score_low, key3, precision=highest).reshape(TOKENS, feature_width)
        dkey = jnp.einsum('htu,thd->uhd', score_low, query3, precision=highest).reshape(TOKENS, feature_width)
        dvalue = jnp.einsum('htu,thd->uhd', prob_low, grad3, precision=highest).reshape(TOKENS, feature_width)
        widened = reduced_in.astype(jnp.float32)
        grad_query = jnp.dot(widened.T, dquery, precision=highest)
        grad_key = jnp.dot(widened.T, dkey, precision=highest)
        grad_value = jnp.dot(widened.T, dvalue, precision=highest)
        grad_output = jnp.dot(reduced_grad.T, out_seq, preferred_element_type=jnp.float32)
        return (totals + jnp.stack([grad_query, grad_key, grad_value, grad_output]), None)
    initial = jnp.zeros((4, RANK, feature_width), jnp.float32)
    result, unused = lax.scan(one_sequence, initial, (layer_input, queries, key_rows, value_rows, attn_out, out_grad, layer_grad, logsum))
    return result
```

```python
import functools
import math

import jax
import jax.numpy as jnp
from jax import lax
from jax.experimental import pallas as pl
from jax.experimental.pallas import tpu as pltpu
from jax.sharding import PartitionSpec as P

BLOCK = 128
DEPTH = 512
CHUNKS = 2
MESH = pl.DeviceIdType.MESH
LOW, WIDE = jnp.bfloat16, jnp.float32


def dot(left, right, dims):
    return lax.dot_general(left, right, (dims, ((), ())), preferred_element_type=jnp.float32)


def value_products(arrays, head, sums, prob_ref, dv_low):
    q_ref, k_ref, g_ref = (arrays.at[index, head] for index in range(3))
    tokens, width = q_ref.shape
    scaling = 1.0 / math.sqrt(width)
    row = lax.broadcasted_iota(jnp.int32, (BLOCK, BLOCK), 0)
    col = lax.broadcasted_iota(jnp.int32, (BLOCK, BLOCK), 1)
    causal = row <= col
    for start in range(0, tokens, BLOCK):
        span = slice(start, start + BLOCK)
        scores = dot(k_ref[span], q_ref[start:], ((1,), (1,))) * scaling
        prob = jnp.exp(scores - sums[:, start:])
        diagonal = jnp.where(causal, prob[:, :BLOCK], 0.0)
        if start + BLOCK < tokens:
            prob = jnp.concatenate([diagonal, prob[:, BLOCK:]], axis=1)
        else:
            prob = diagonal
        prob_ref[span, start:] = prob
        dv_low[span] = dot(prob.astype(LOW), g_ref[start:], ((1,), (0,))).astype(LOW)


def score_products(arrays, head, deltas, prob_ref, acc, qk_low):
    q_ref, k_ref, g_ref, v_ref = (arrays.at[index, head] for index in range(4))
    tokens, width = q_ref.shape
    scaling = 1.0 / math.sqrt(width)
    for start in range(0, tokens, BLOCK):
        span = slice(start, start + BLOCK)
        dprob = dot(v_ref[span], g_ref[start:], ((1,), (1,)))
        dscore = prob_ref[span, start:] * (dprob - deltas[:, start:]) * scaling
        score_low = dscore.astype(LOW)
        dquery = dot(score_low, k_ref[span], ((0,), (0,)))
        if start == 0:
            acc[...] = dquery
        else:
            acc[start:] += dquery
        qk_low[span, :width] = acc[span].astype(LOW)
        qk_low[span, width:] = dot(score_low, q_ref[start:], ((1,), (0,))).astype(LOW)


def kernel(
    dp_size,
    ctx_size,
    layer_input,
    q_hbm,
    k_hbm,
    v_hbm,
    o_hbm,
    g_hbm,
    layer_grad,
    sums_ref,
    projector,
    out_ref,
    arrays,
    rows_in,
    proj,
    proj_acc,
    grad_own,
    out_own,
    reduced,
    reduced_t,
    reduced_grad,
    delta_out,
    delta_in,
    delta_rows,
    prob_ref,
    acc,
    dv_low,
    qk_low,
    mine_v,
    core_out_v,
    core_in_v,
    core_out_qk,
    core_in_qk,
    total_ref,
    far_out,
    far_in,
    final_own,
    final_out,
    final_in,
    last_own_v,
    last_out_v,
    last_in_v,
    last_own_qk,
    last_out_qk,
    last_in_qk,
    own_o,
    sum_out_o,
    sum_in_o,
    final_own_o,
    final_out_o,
    final_in_o,
    load_sem,
    local_sem,
    head_send,
    head_recv,
    red_send,
    red_recv,
    pass_send,
    pass_recv,
    delta_send,
    delta_recv,
    core_send,
    core_recv,
    far_send,
    far_recv,
    final_send,
    final_recv,
    last_send,
    last_recv,
    sum_send_o,
    sum_recv_o,
    final_send_o,
    final_recv_o,
):
    me = lax.axis_index("ctx")
    place = lax.axis_index("dp")
    bits = dp_size.bit_length() - 1
    fars = dp_size // 2
    core = lax.rem(place, 2)
    far = place // 2
    sources = (q_hbm, k_hbm, g_hbm, v_hbm)
    count = len(sources)
    heads = arrays.shape[1]
    last = heads - 1
    rows = q_hbm.shape[0]
    width = arrays.shape[3]
    depth = projector.shape[0]
    rank = projector.shape[1]
    piece = rank // dp_size
    slab = piece // ctx_size
    both = 2 * width
    passing = ctx_size == 4
    mine = pl.ds(pl.multiple_of(me * rows, 16), rows)
    ctx_steps = range(1, ctx_size)

    def columns(owner, head):
        return pl.ds(pl.multiple_of((owner * heads + head) * width, width), width)

    def remote(src, dst, send, recv, **where):
        return pltpu.make_async_remote_copy(
            src_ref=src,
            dst_ref=dst,
            send_sem=send,
            recv_sem=recv,
            device_id=where,
            device_id_type=MESH,
        )

    def local_copy(head, index):
        return pltpu.make_async_copy(
            sources[index].at[:, columns(me, head)],
            arrays.at[index, head, mine],
            local_sem.at[head, index],
        )

    def head_copy(head, index, d):
        peer = me ^ d
        return remote(
            sources[index].at[:, columns(peer, head)],
            arrays.at[index, head, mine],
            head_send.at[head, index, d - 1],
            head_recv.at[head, index, d - 1],
            ctx=peer,
        )

    def start_head(head, indices):
        for index in indices:
            for d in ctx_steps:
                head_copy(head, index, d).start()
        for index in indices:
            local_copy(head, index).start()

    def wait_head(head, indices):
        for index in indices:
            local_copy(head, index).wait()
            for d in ctx_steps:
                head_copy(head, index, d).wait_recv()

    red_steps = (1, 2) if passing else tuple(ctx_steps)

    def reduced_copy(d):
        return remote(
            reduced.at[mine],
            reduced.at[mine],
            red_send.at[d - 1],
            red_recv.at[d - 1],
            ctx=me ^ d,
        )

    def pass_copy(d):
        half = rows // 2
        at = pl.ds(pl.multiple_of((me ^ d) * rows + (d - 1) * half, 16), half)
        return remote(
            reduced.at[at],
            reduced.at[at],
            pass_send.at[d - 1],
            pass_recv.at[d - 1],
            ctx=me ^ (3 - d),
        )

    def delta_copy(d):
        peer = me ^ d
        return remote(
            delta_out.at[peer],
            delta_in.at[me],
            delta_send.at[d - 1],
            delta_recv.at[d - 1],
            ctx=peer,
        )

    def core_copy(head, part):
        out, arrived = ((core_out_v, core_in_v), (core_out_qk, core_in_qk))[part]
        return remote(
            out.at[head],
            arrived.at[head],
            core_send.at[head, part],
            core_recv.at[head, part],
            dp=place ^ 1,
        )

    def far_copy(head, d):
        return remote(
            far_out.at[head, far ^ d],
            far_in.at[head, d - 1],
            far_send.at[head, d - 1],
            far_recv.at[head, d - 1],
            dp=place ^ (2 * d),
        )

    def final_copy(head, d):
        peer = me ^ d
        return remote(
            final_out.at[head, peer],
            final_in.at[head, d - 1],
            final_send.at[head, d - 1],
            final_recv.at[head, d - 1],
            ctx=peer,
        )

    def last_copy(part, f, d):
        out, arrived = ((last_out_v, last_in_v), (last_out_qk, last_in_qk))[part]
        return remote(
            out.at[far ^ f, me ^ d],
            arrived.at[f, d],
            last_send.at[part, f, d],
            last_recv.at[part, f, d],
            dp=place ^ (2 * f),
            ctx=me ^ d,
        )

    last_steps = [
        (f, d) for f in reversed(range(fars)) for d in reversed(range(ctx_size)) if f or d
    ]

    def group_o(chunk):
        return tuple(ref.at[chunk] for ref in (own_o, sum_out_o, sum_in_o, sum_send_o, sum_recv_o))

    def place_bit(stage):
        return lax.rem(place // 2**stage, 2)

    def stage_copy(group, stage):
        half = dp_size // 2 ** (stage + 1)
        span = pl.ds(dp_size - 2 * half, half)
        return remote(
            group[1].at[span],
            group[2].at[span],
            group[3].at[stage],
            group[4].at[stage],
            dp=place ^ 2**stage,
        )

    def stage_blocks(stage, bit):
        half = dp_size // 2 ** (stage + 1)
        first = lax.rem(place, 2**stage) + bit * 2**stage
        return [(first + 2 ** (stage + 1) * j, dp_size - 2 * half + j) for j in range(half)]

    def send_stage(group, stage):
        for block, slot in stage_blocks(stage, 1 - place_bit(stage)):
            group[1][slot] = group[0][block].astype(LOW)
        stage_copy(group, stage).start()

    def add_stage(group, stage):
        stage_copy(group, stage).wait_recv()
        for block, slot in stage_blocks(stage, place_bit(stage)):
            group[0][block] += group[2][slot].astype(WIDE)

    def final_copy_o(chunk, d):
        peer = me ^ d
        return remote(
            final_out_o.at[chunk, peer],
            final_in_o.at[chunk, d - 1],
            final_send_o.at[chunk, d - 1],
            final_recv_o.at[chunk, d - 1],
            ctx=peer,
        )

    def advance_o(chunk, stage):
        group = group_o(chunk)
        add_stage(group, stage)
        if stage + 1 < bits:
            send_stage(group, stage + 1)
            return
        total = own_o[chunk, place]
        for to in range(ctx_size):
            part = total[to * slab : (to + 1) * slab]
            final_own_o[chunk, to] = part
            final_out_o[chunk, to] = part.astype(LOW)
        for d in ctx_steps:
            final_copy_o(chunk, d).start()

    loads = (
        pltpu.make_async_copy(projector, proj, load_sem.at[0]),
        pltpu.make_async_copy(layer_input, rows_in.at[:rows], load_sem.at[1]),
        pltpu.make_async_copy(layer_grad, rows_in.at[rows:], load_sem.at[2]),
        pltpu.make_async_copy(o_hbm, out_own, load_sem.at[3]),
        pltpu.make_async_copy(g_hbm, grad_own, load_sem.at[4]),
    )
    barrier = pltpu.get_barrier_semaphore()
    for d in ctx_steps:
        pl.semaphore_signal(barrier, inc=1, device_id={"ctx": me ^ d}, device_id_type=MESH)
    for stage in range(bits):
        peer = place ^ 2**stage
        pl.semaphore_signal(barrier, inc=1, device_id={"dp": peer}, device_id_type=MESH)
    for load in loads:
        load.start()
    pl.semaphore_wait(barrier, ctx_size - 1 + bits)

    start_head(0, range(count))
    for load in loads[:3]:
        load.wait()
    proj_acc[...] = jnp.zeros_like(proj_acc)

    @pl.loop(0, depth // DEPTH)
    def _(step):
        at = pl.ds(pl.multiple_of(step * DEPTH, DEPTH), DEPTH)
        proj_acc[...] += dot(rows_in[:, at], proj[at], ((1,), (0,)))

    reduced[mine] = proj_acc[:rows].astype(LOW)
    for d in red_steps:
        reduced_copy(d).start()
    start_head(1, range(2))
    reduced_grad[...] = proj_acc[rows:].astype(LOW)
    for load in loads[3:]:
        load.wait()
    rgrad_t = reduced_grad[...].T
    part_width = own_o.shape[3]
    for chunk in range(CHUNKS):
        at = slice(chunk * part_width, (chunk + 1) * part_width)
        for part in range(dp_size):
            span = slice(part * piece, (part + 1) * piece)
            own_o[chunk, part] = dot(rgrad_t[span], out_own[:, at], ((1,), (0,)))
        send_stage(group_o(chunk), 0)

    lane = lax.broadcasted_iota(jnp.int32, (rows, BLOCK), 1)
    table = jnp.zeros((rows, BLOCK), WIDE)
    for head in range(heads * ctx_size):
        span = slice(head * width, (head + 1) * width)
        product = grad_own[:, span].astype(WIDE) * out_own[:, span].astype(WIDE)
        table = jnp.where(lane == head, jnp.sum(product, axis=1, keepdims=True), table)
    table = table.T
    delta_out[...] = jnp.zeros_like(delta_out)
    for owner in range(ctx_size):
        delta_out[owner, :heads] = table[owner * heads : (owner + 1) * heads]
    delta_in[me] = delta_out[me]
    for d in ctx_steps:
        delta_copy(d).start()
    for chunk in range(CHUNKS):
        advance_o(chunk, 0)

    pending = [(chunk, stage) for stage in range(1, bits) for chunk in range(CHUNKS)]

    def gather_reduced():
        for d in red_steps:
            reduced_copy(d).wait_recv()
            if passing:
                pass_copy(d).start()
        start_head(1, range(2, count))
        for head in range(2, heads):
            start_head(head, range(count))
        for item in pending[:1]:
            advance_o(*item)
        for d in ctx_steps:
            delta_copy(d).wait_recv()
        delta_rows[...] = jnp.concatenate([delta_in[owner] for owner in range(ctx_size)], axis=1)
        if passing:
            for d in red_steps:
                pass_copy(d).wait_recv()
        turned = reduced[...].T
        for part in range(dp_size):
            block = turned[part * piece : (part + 1) * piece]
            reduced_t[part % 2, (part // 2) * piece : (part // 2 + 1) * piece] = block

    def keep(head, total, lanes):
        for f in range(fars):
            block = total[f * piece : (f + 1) * piece]
            total_ref[head, f, :, lanes] = block
            far_out[head, f, :, lanes] = block.astype(LOW)

    def send_last(total, part):
        own, out = ((last_own_v, last_out_v), (last_own_qk, last_out_qk))[part]
        for f in range(fars):
            for to in range(ctx_size):
                first = f * piece + to * slab
                block = total[first : first + slab]
                own[f, to] = block
                out[f, to] = block.astype(LOW)
        for f, d in last_steps:
            last_copy(part, f, d).start()

    def finish(head):
        total = total_ref[head, far]
        for d in range(1, fars):
            far_copy(head, d).wait_recv()
            total += far_in[head, d - 1].astype(WIDE)
        for to in range(ctx_size):
            block = total[to * slab : (to + 1) * slab]
            final_own[head, to] = block
            final_out[head, to] = block.astype(LOW)
        for d in ctx_steps:
            final_copy(head, d).start()

    @pl.loop(0, heads)
    def _(head):
        wait_head(head, range(3))
        sums = sums_ref[pl.ds(me * heads + head, 1), :]
        value_products(arrays, head, sums, prob_ref, dv_low)

        @pl.when(head == 0)
        def _():
            gather_reduced()

        low = dv_low[...]
        core_out_v[head] = dot(reduced_t[1 - core], low, ((1,), (0,))).astype(LOW)
        core_copy(head, 0).start()
        mine_v[...] = dot(reduced_t[core], low, ((1,), (0,)))
        core_copy(head, 0).wait_recv()
        total = mine_v[...] + core_in_v[head].astype(WIDE)

        @pl.when(head < last)
        def _():
            keep(head, total, slice(both, both + width))

        @pl.when(head == last)
        def _():
            send_last(total, 0)

        wait_head(head, range(3, count))
        score_products(arrays, head, delta_rows[pl.ds(head, 1), :], prob_ref, acc, qk_low)
        low = qk_low[...]
        core_out_qk[head] = dot(reduced_t[1 - core], low, ((1,), (0,))).astype(LOW)
        core_copy(head, 1).start()
        joined = dot(reduced_t[core], low, ((1,), (0,)))
        core_copy(head, 1).wait_recv()
        total = joined + core_in_qk[head].astype(WIDE)

        @pl.when(head < last)
        def _():
            keep(head, total, slice(0, both))
            for d in reversed(range(1, fars)):
                far_copy(head, d).start()

        @pl.when(head == last)
        def _():
            send_last(total, 1)

        @pl.when(head > 0)
        def _():
            finish(head - 1)

        @pl.when(head == 0)
        def _():
            for item in pending[1:2]:
                advance_o(*item)

        @pl.when(head == max(last - 1, 0))
        def _():
            for item in pending[2:]:
                advance_o(*item)

    for d in red_steps:
        reduced_copy(d).wait_send()
    if passing:
        for d in red_steps:
            pass_copy(d).wait_send()
    for d in ctx_steps:
        delta_copy(d).wait_send()
    for chunk in range(CHUNKS):
        for stage in range(bits):
            stage_copy(group_o(chunk), stage).wait_send()
    for head in range(heads):
        for part in range(2):
            core_copy(head, part).wait_send()
        for index in range(count):
            for d in ctx_steps:
                head_copy(head, index, d).wait_send()

    for chunk in range(CHUNKS):
        at = slice(chunk * part_width, (chunk + 1) * part_width)
        total = final_own_o[chunk, me]
        for d in ctx_steps:
            final_copy_o(chunk, d).wait()
            total += final_in_o[chunk, d - 1].astype(WIDE)
        out_ref[3, :, at] = total

    for head in range(last):
        for d in range(1, fars):
            far_copy(head, d).wait_send()
        for d in range(ctx_size):
            if d:
                final_copy(head, d).wait()
                block = final_in[head, d - 1].astype(WIDE)
            else:
                block = final_own[head, me]
            for index in range(3):
                span = slice(index * width, (index + 1) * width)
                out_ref[index, :, columns(me ^ d, head)] = block[:, span]

    for part, own, arrived, first in ((0, last_own_v, last_in_v, 2), (1, last_own_qk, last_in_qk, 0)):
        for f, d in last_steps:
            last_copy(part, f, d).wait()
        for d in range(ctx_size):
            total = None if d else own[far, me]
            for f in range(fars):
                if f or d:
                    block = arrived[f, d].astype(WIDE)
                    total = block if total is None else total + block
            for index in range(own.shape[3] // width):
                span = slice(index * width, (index + 1) * width)
                out_ref[first + index, :, columns(me ^ d, last)] = total[:, span]


def on_device(
    dp_size,
    ctx_size,
    layer_input,
    queries,
    key_rows,
    value_rows,
    attn_out,
    out_grad,
    layer_grad,
    logsum,
    projector,
):
    rows, features = queries.shape[1:]
    all_heads, tokens = logsum.shape[1:]
    heads = all_heads // ctx_size
    width = features // all_heads
    depth, rank = projector.shape
    bits = dp_size.bit_length() - 1
    fars = dp_size // 2
    piece = rank // dp_size
    slab = piece // ctx_size
    padded = -(-heads // 8) * 8
    half = rank // 2
    both = 2 * width
    three = 3 * width
    part_width = features // CHUNKS
    others = ctx_size - 1
    dma = pltpu.SemaphoreType.DMA
    anywhere = pl.BlockSpec(memory_space=pl.ANY)
    in_vmem = pl.BlockSpec(memory_space=pltpu.VMEM)
    return pl.pallas_call(
        functools.partial(kernel, dp_size, ctx_size),
        out_shape=jax.ShapeDtypeStruct((4, slab, features), WIDE),
        in_specs=[anywhere] * 7 + [in_vmem, anywhere],
        out_specs=in_vmem,
        scratch_shapes=[
            pltpu.VMEM((4, heads, tokens, width), LOW),
            pltpu.VMEM((2 * rows, depth), LOW),
            pltpu.VMEM((depth, rank), LOW),
            pltpu.VMEM((2 * rows, rank), WIDE),
            pltpu.VMEM((rows, features), LOW),
            pltpu.VMEM((rows, features), LOW),
            pltpu.VMEM((tokens, rank), LOW),
            pltpu.VMEM((2, half, tokens), LOW),
            pltpu.VMEM((rows, rank), LOW),
            pltpu.VMEM((ctx_size, padded, rows), WIDE),
            pltpu.VMEM((ctx_size, padded, rows), WIDE),
            pltpu.VMEM((padded, tokens), WIDE),
            pltpu.VMEM((tokens, tokens), WIDE),
            pltpu.VMEM((tokens, width), WIDE),
            pltpu.VMEM((tokens, width), LOW),
            pltpu.VMEM((tokens, both), LOW),
            pltpu.VMEM((half, width), WIDE),
            pltpu.VMEM((heads, half, width), LOW),
            pltpu.VMEM((heads, half, width), LOW),
            pltpu.VMEM((heads, half, both), LOW),
            pltpu.VMEM((heads, half, both), LOW),
            pltpu.VMEM((heads, fars, piece, three), WIDE),
            pltpu.VMEM((heads, fars, piece, three), LOW),
            pltpu.VMEM((heads, fars - 1, piece, three), LOW),
            pltpu.VMEM((heads, ctx_size, slab, three), WIDE),
            pltpu.VMEM((heads, ctx_size, slab, three), LOW),
            pltpu.VMEM((heads, others, slab, three), LOW),
            pltpu.VMEM((fars, ctx_size, slab, width), WIDE),
            pltpu.VMEM((fars, ctx_size, slab, width), LOW),
            pltpu.VMEM((fars, ctx_size, slab, width), LOW),
            pltpu.VMEM((fars, ctx_size, slab, both), WIDE),
            pltpu.VMEM((fars, ctx_size, slab, both), LOW),
            pltpu.VMEM((fars, ctx_size, slab, both), LOW),
            pltpu.VMEM((CHUNKS, dp_size, piece, part_width), WIDE),
            pltpu.VMEM((CHUNKS, dp_size - 1, piece, part_width), LOW),
            pltpu.VMEM((CHUNKS, dp_size - 1, piece, part_width), LOW),
            pltpu.VMEM((CHUNKS, ctx_size, slab, part_width), WIDE),
            pltpu.VMEM((CHUNKS, ctx_size, slab, part_width), LOW),
            pltpu.VMEM((CHUNKS, others, slab, part_width), LOW),
            dma((5,)),
            dma((heads, 4)),
            dma((heads, 4, others)),
            dma((heads, 4, others)),
            dma((others,)),
            dma((others,)),
            dma((2,)),
            dma((2,)),
            dma((others,)),
            dma((others,)),
            dma((heads, 2)),
            dma((heads, 2)),
            dma((heads, fars - 1)),
            dma((heads, fars - 1)),
            dma((heads, others)),
            dma((heads, others)),
            dma((2, fars, ctx_size)),
            dma((2, fars, ctx_size)),
            dma((CHUNKS, bits)),
            dma((CHUNKS, bits)),
            dma((CHUNKS, others)),
            dma((CHUNKS, others)),
        ],
        compiler_params=pltpu.CompilerParams(
            collective_id=0, has_side_effects=True, vmem_limit_bytes=56 * 1024 * 1024
        ),
    )(
        layer_input[0],
        queries[0],
        key_rows[0],
        value_rows[0],
        attn_out[0],
        out_grad[0],
        layer_grad[0],
        logsum[0],
        projector,
    )


def solution(mesh):
    rows = P("dp", "ctx", None)
    placed = (rows,) * 7 + (P("dp", None, None), P())
    return jax.shard_map(
        functools.partial(on_device, mesh.shape["dp"], mesh.shape["ctx"]),
        mesh=mesh,
        in_specs=placed,
        out_specs=P(None, ("dp", "ctx"), None),
        check_vma=False,
    )
```

```python
import functools
import math

import jax
import jax.numpy as jnp
from jax import lax
from jax.experimental import pallas as pl
from jax.experimental.pallas import tpu as pltpu
from jax.sharding import PartitionSpec as P

BLOCK = 128
DEPTH = 512
CHUNKS = 4
MESH = pl.DeviceIdType.MESH
LOW, WIDE = jnp.bfloat16, jnp.float32


def dot(left, right, dims):
    return lax.dot_general(left, right, (dims, ((), ())), preferred_element_type=jnp.float32)


def value_products(arrays, head, sums, prob_ref, dv_low):
    q_ref, k_ref, g_ref = (arrays.at[index, head] for index in range(3))
    tokens, width = q_ref.shape
    scaling = 1.0 / math.sqrt(width)
    row = lax.broadcasted_iota(jnp.int32, (BLOCK, BLOCK), 0)
    col = lax.broadcasted_iota(jnp.int32, (BLOCK, BLOCK), 1)
    causal = row <= col
    for start in range(0, tokens, BLOCK):
        span = slice(start, start + BLOCK)
        scores = dot(k_ref[span], q_ref[start:], ((1,), (1,))) * scaling
        prob = jnp.exp(scores - sums[:, start:])
        diagonal = jnp.where(causal, prob[:, :BLOCK], 0.0)
        if start + BLOCK < tokens:
            prob = jnp.concatenate([diagonal, prob[:, BLOCK:]], axis=1)
        else:
            prob = diagonal
        prob_ref[span, start:] = prob
        dv_low[span] = dot(prob.astype(LOW), g_ref[start:], ((1,), (0,))).astype(LOW)


def score_products(arrays, head, deltas, prob_ref, acc, qk_low, between):
    q_ref, k_ref, g_ref, v_ref = (arrays.at[index, head] for index in range(4))
    tokens, width = q_ref.shape
    scaling = 1.0 / math.sqrt(width)
    for start in range(0, tokens, BLOCK):
        span = slice(start, start + BLOCK)
        dprob = dot(v_ref[span], g_ref[start:], ((1,), (1,)))
        dscore = prob_ref[span, start:] * (dprob - deltas[:, start:]) * scaling
        score_low = dscore.astype(LOW)
        dquery = dot(score_low, k_ref[span], ((0,), (0,)))
        if start == 0:
            acc[...] = dquery
        else:
            acc[start:] += dquery
        qk_low[span, :width] = acc[span].astype(LOW)
        qk_low[span, width:] = dot(score_low, q_ref[start:], ((1,), (0,))).astype(LOW)
        if start == BLOCK:
            between()


def kernel(
    dp_size,
    ctx_size,
    layer_input,
    q_hbm,
    k_hbm,
    v_hbm,
    o_hbm,
    g_hbm,
    layer_grad,
    sums_ref,
    projector,
    out_ref,
    arrays,
    rows_in,
    proj,
    proj_acc,
    grad_own,
    out_own,
    reduced,
    reduced_t,
    reduced_grad,
    delta_out,
    delta_in,
    delta_rows,
    prob_ref,
    acc,
    dv_low,
    qk_low,
    mine_v,
    core_out_v,
    core_in_v,
    core_out_qk,
    core_in_qk,
    total_ref,
    far_out,
    far_in,
    final_own,
    final_out,
    final_in,
    last_own_v,
    last_out_v,
    last_in_v,
    last_own_qk,
    last_out_qk,
    last_in_qk,
    own_o,
    sum_out_o,
    sum_in_o,
    final_own_o,
    final_out_o,
    final_in_o,
    load_sem,
    local_sem,
    head_send,
    head_recv,
    red_send,
    red_recv,
    pass_send,
    pass_recv,
    delta_send,
    delta_recv,
    core_send,
    core_recv,
    far_send,
    far_recv,
    final_send,
    final_recv,
    last_send,
    last_recv,
    sum_send_o,
    sum_recv_o,
    final_send_o,
    final_recv_o,
    known,
):
    me = lax.axis_index("ctx")
    place = lax.axis_index("dp")
    bits = dp_size.bit_length() - 1
    fars = dp_size // 2
    core = lax.rem(place, 2)
    far = place // 2
    sources = (q_hbm, k_hbm, g_hbm, v_hbm)
    count = len(sources)
    heads = arrays.shape[1]
    last = heads - 1
    rows = q_hbm.shape[0]
    width = arrays.shape[3]
    depth = projector.shape[0]
    rank = projector.shape[1]
    piece = rank // dp_size
    slab = piece // ctx_size
    both = 2 * width
    passing = ctx_size == 4
    near = ctx_size == 4 and fars == 4
    mine = pl.ds(pl.multiple_of(me * rows, 16), rows)
    ctx_steps = range(1, ctx_size)

    def columns(owner, head):
        return pl.ds(pl.multiple_of((owner * heads + head) * width, width), width)

    def remote(src, dst, send, recv, **where):
        return pltpu.make_async_remote_copy(
            src_ref=src,
            dst_ref=dst,
            send_sem=send,
            recv_sem=recv,
            device_id=where,
            device_id_type=MESH,
        )

    def local_copy(head, index):
        return pltpu.make_async_copy(
            sources[index].at[:, columns(me, head)],
            arrays.at[index, head, mine],
            local_sem.at[head, index],
        )

    def head_copy(head, index, d):
        peer = me ^ d
        return remote(
            sources[index].at[:, columns(peer, head)],
            arrays.at[index, head, mine],
            head_send.at[head, index, d - 1],
            head_recv.at[head, index, d - 1],
            ctx=peer,
        )

    def start_head(head, indices):
        for index in indices:
            for d in ctx_steps:
                head_copy(head, index, d).start()
        for index in indices:
            local_copy(head, index).start()

    def wait_sent(head):
        for index in range(count):
            for d in ctx_steps:
                head_copy(head, index, d).wait_send()

    def wait_head(head, indices):
        for index in indices:
            local_copy(head, index).wait()
            for d in ctx_steps:
                head_copy(head, index, d).wait_recv()

    red_steps = (1, 2) if passing else tuple(ctx_steps)

    def reduced_copy(d):
        return remote(
            reduced.at[mine],
            reduced.at[mine],
            red_send.at[d - 1],
            red_recv.at[d - 1],
            ctx=me ^ d,
        )

    def pass_copy(d):
        half = rows // 2
        at = pl.ds(pl.multiple_of((me ^ d) * rows + (d - 1) * half, 16), half)
        return remote(
            reduced.at[at],
            reduced.at[at],
            pass_send.at[d - 1],
            pass_recv.at[d - 1],
            ctx=me ^ (3 - d),
        )

    def delta_copy(d):
        peer = me ^ d
        return remote(
            delta_out.at[peer],
            delta_in.at[me],
            delta_send.at[d - 1],
            delta_recv.at[d - 1],
            ctx=peer,
        )

    def core_copy(head, part):
        out, arrived = ((core_out_v, core_in_v), (core_out_qk, core_in_qk))[part]
        return remote(
            out.at[head],
            arrived.at[head],
            core_send.at[head, part],
            core_recv.at[head, part],
            dp=place ^ 1,
        )

    def far_copy(head, d):
        return remote(
            far_out.at[head, far ^ d],
            far_in.at[head, d - 1],
            far_send.at[head, d - 1],
            far_recv.at[head, d - 1],
            dp=place ^ (2 * d),
        )

    def final_copy(head, d):
        peer = me ^ d
        return remote(
            final_out.at[head, peer],
            final_in.at[head, d - 1],
            final_send.at[head, d - 1],
            final_recv.at[head, d - 1],
            ctx=peer,
        )

    def last_copy(part, f, d):
        out, arrived = ((last_out_v, last_in_v), (last_out_qk, last_in_qk))[part]
        return remote(
            out.at[(far ^ f) * ctx_size + (me ^ d)],
            arrived.at[f * ctx_size + d],
            last_send.at[part],
            last_recv.at[part],
            dp=place ^ (2 * f),
            ctx=me ^ d,
        )

    def wait_last(part):
        arrived = (last_in_v, last_in_qk)[part]
        all_others = arrived.at[pl.ds(1, fars * ctx_size - 1)]
        for sem in (last_recv, last_send):
            pltpu.make_async_copy(all_others, all_others, sem.at[part]).wait()

    last_steps = [
        (f, d) for f in reversed(range(fars)) for d in reversed(range(ctx_size)) if f or d
    ]

    def group_o(chunk):
        return tuple(ref.at[chunk] for ref in (own_o, sum_out_o, sum_in_o, sum_send_o, sum_recv_o))

    def place_bit(stage):
        return lax.rem(place // 2**stage, 2)

    def stage_copy(group, stage):
        half = dp_size // 2 ** (stage + 1)
        span = pl.ds(dp_size - 2 * half, half)
        return remote(
            group[1].at[span],
            group[2].at[span],
            group[3].at[stage],
            group[4].at[stage],
            dp=place ^ 2**stage,
        )

    def stage_blocks(stage, bit):
        half = dp_size // 2 ** (stage + 1)
        first = lax.rem(place, 2**stage) + bit * 2**stage
        return [(first + 2 ** (stage + 1) * j, dp_size - 2 * half + j) for j in range(half)]

    def send_stage(group, stage):
        for block, slot in stage_blocks(stage, 1 - place_bit(stage)):
            group[1][slot] = group[0][block].astype(LOW)
        stage_copy(group, stage).start()

    def add_stage(group, stage):
        stage_copy(group, stage).wait_recv()
        for block, slot in stage_blocks(stage, place_bit(stage)):
            group[0][block] += group[2][slot].astype(WIDE)

    def final_copy_o(chunk, d):
        peer = me ^ d
        return remote(
            final_out_o.at[chunk, peer],
            final_in_o.at[chunk, d - 1],
            final_send_o.at[chunk, d - 1],
            final_recv_o.at[chunk, d - 1],
            ctx=peer,
        )

    def advance_o(chunk, stage):
        group = group_o(chunk)
        add_stage(group, stage)
        if stage + 1 < bits:
            send_stage(group, stage + 1)
            return
        total = own_o[chunk, place]
        for to in range(ctx_size):
            part = total[to * slab : (to + 1) * slab]
            final_own_o[chunk, to] = part
            final_out_o[chunk, to] = part.astype(LOW)
        for d in ctx_steps:
            final_copy_o(chunk, d).start()

    loads = (
        pltpu.make_async_copy(projector, proj, load_sem.at[0]),
        pltpu.make_async_copy(layer_input, rows_in.at[:rows], load_sem.at[1]),
        pltpu.make_async_copy(layer_grad, rows_in.at[rows:], load_sem.at[2]),
        pltpu.make_async_copy(o_hbm, out_own, load_sem.at[3]),
        pltpu.make_async_copy(g_hbm, grad_own, load_sem.at[4]),
    )
    barrier = pltpu.get_barrier_semaphore()
    greet_ctx = (1, 2) if near else tuple(ctx_steps)
    greet_dp = (0,) if near else tuple(range(bits))
    for d in greet_ctx:
        pl.semaphore_signal(barrier, inc=1, device_id={"ctx": me ^ d}, device_id_type=MESH)
    for stage in greet_dp:
        peer = place ^ 2**stage
        pl.semaphore_signal(barrier, inc=1, device_id={"dp": peer}, device_id_type=MESH)
    if near:

        @pl.when(far > 0)
        def _():
            pl.semaphore_signal(barrier, inc=1, device_id={"dp": place - 2}, device_id_type=MESH)

        @pl.when(far < fars - 1)
        def _():
            pl.semaphore_signal(barrier, inc=1, device_id={"dp": place + 2}, device_id_type=MESH)

    for load in loads:
        load.start()
    greeted = len(greet_ctx) + len(greet_dp)
    if near:
        inner = jnp.logical_and(far > 0, far < fars - 1)
        pl.semaphore_wait(barrier, greeted + 1 + inner.astype(jnp.int32))
        for index in range(2):
            for d in (1, 2):
                head_copy(0, index, d).start()
        pl.semaphore_signal(known.at[0], inc=1, device_id={"ctx": me ^ 1}, device_id_type=MESH)

        @pl.when(inner)
        def _():
            for step in (-2, 2):
                pl.semaphore_signal(
                    known.at[1], inc=1, device_id={"dp": place + step}, device_id_type=MESH
                )

        pl.semaphore_wait(known.at[0], 1)
        for index in range(2):
            head_copy(0, index, 3).start()
            local_copy(0, index).start()
        start_head(0, range(2, count))
    else:
        pl.semaphore_wait(barrier, greeted)
        start_head(0, range(count))
    for load in loads[:3]:
        load.wait()
    proj_acc[...] = jnp.zeros_like(proj_acc)

    @pl.loop(0, depth // DEPTH)
    def _(step):
        at = pl.ds(pl.multiple_of(step * DEPTH, DEPTH), DEPTH)
        proj_acc[...] += dot(rows_in[:, at], proj[at], ((1,), (0,)))

    reduced[mine] = proj_acc[:rows].astype(LOW)
    for d in red_steps:
        reduced_copy(d).start()
    start_head(1, range(2))
    reduced_grad[...] = proj_acc[rows:].astype(LOW)
    for load in loads[3:]:
        load.wait()
    rgrad_t = reduced_grad[...].T
    part_width = own_o.shape[3]
    for chunk in range(CHUNKS):
        at = slice(chunk * part_width, (chunk + 1) * part_width)
        for part in range(dp_size):
            span = slice(part * piece, (part + 1) * piece)
            own_o[chunk, part] = dot(rgrad_t[span], out_own[:, at], ((1,), (0,)))
        send_stage(group_o(chunk), 0)

    lane = lax.broadcasted_iota(jnp.int32, (rows, BLOCK), 1)
    table = jnp.zeros((rows, BLOCK), WIDE)
    for head in range(heads * ctx_size):
        span = slice(head * width, (head + 1) * width)
        product = grad_own[:, span].astype(WIDE) * out_own[:, span].astype(WIDE)
        table = jnp.where(lane == head, jnp.sum(product, axis=1, keepdims=True), table)
    table = table.T
    delta_out[...] = jnp.zeros_like(delta_out)
    for owner in range(ctx_size):
        delta_out[owner, :heads] = table[owner * heads : (owner + 1) * heads]
    delta_in[me] = delta_out[me]
    for d in ctx_steps:
        delta_copy(d).start()
    for chunk in range(2):
        advance_o(chunk, 0)

    def complete_o(chunks):
        for chunk in chunks:
            for stage in range(2, bits):
                advance_o(chunk, stage)

    def gather_reduced():
        if near:
            pl.semaphore_wait(known.at[1], 1)
        advance_o(0, 1)
        advance_o(2, 0)
        for d in red_steps:
            reduced_copy(d).wait_recv()
            if passing:
                pass_copy(d).start()
        start_head(1, range(2, count))
        for head in range(2, heads):
            start_head(head, range(count))
        advance_o(1, 1)
        advance_o(3, 0)
        for d in ctx_steps:
            delta_copy(d).wait_recv()
        delta_rows[...] = jnp.concatenate([delta_in[owner] for owner in range(ctx_size)], axis=1)
        advance_o(2, 1)
        if passing:
            for d in red_steps:
                pass_copy(d).wait_recv()
        turned = reduced[...].T
        for part in range(dp_size):
            block = turned[part * piece : (part + 1) * piece]
            reduced_t[part % 2, (part // 2) * piece : (part // 2 + 1) * piece] = block

    def keep(head, total, lanes):
        for f in range(fars):
            block = total[f * piece : (f + 1) * piece]
            total_ref[head, f, :, lanes] = block
            far_out[head, f, :, lanes] = block.astype(LOW)

    def send_last(total, part):
        own, out = ((last_own_v, last_out_v), (last_own_qk, last_out_qk))[part]
        for f in range(fars):
            for to in range(ctx_size):
                first = f * piece + to * slab
                block = total[first : first + slab]
                own[f, to] = block
                out[f * ctx_size + to] = block.astype(LOW)
        for f, d in last_steps:
            last_copy(part, f, d).start()

    def finish(head):
        total = total_ref[head, far]
        for d in range(1, fars):
            far_copy(head, d).wait_recv()
            total += far_in[head, d - 1].astype(WIDE)
        for to in range(ctx_size):
            block = total[to * slab : (to + 1) * slab]
            final_own[head, to] = block
            final_out[head, to] = block.astype(LOW)
        for d in ctx_steps:
            final_copy(head, d).start()

    @pl.loop(0, heads)
    def _(head):
        wait_head(head, range(3))
        sums = sums_ref[pl.ds(me * heads + head, 1), :]
        value_products(arrays, head, sums, prob_ref, dv_low)

        @pl.when(head == 0)
        def _():
            gather_reduced()

        low = dv_low[...]
        core_out_v[head] = dot(reduced_t[1 - core], low, ((1,), (0,))).astype(LOW)
        core_copy(head, 0).start()
        mine_v[...] = dot(reduced_t[core], low, ((1,), (0,)))

        def add_values():
            core_copy(head, 0).wait_recv()
            total = mine_v[...] + core_in_v[head].astype(WIDE)

            @pl.when(head < last)
            def _():
                keep(head, total, slice(both, both + width))

            @pl.when(head == last)
            def _():
                send_last(total, 0)

        wait_head(head, range(3, count))
        deltas = delta_rows[pl.ds(head, 1), :]
        score_products(arrays, head, deltas, prob_ref, acc, qk_low, add_values)
        low = qk_low[...]
        core_out_qk[head] = dot(reduced_t[1 - core], low, ((1,), (0,))).astype(LOW)
        core_copy(head, 1).start()
        joined = dot(reduced_t[core], low, ((1,), (0,)))
        core_copy(head, 1).wait_recv()
        total = joined + core_in_qk[head].astype(WIDE)

        @pl.when(head < last)
        def _():
            keep(head, total, slice(0, both))
            for d in reversed(range(1, fars)):
                far_copy(head, d).start()

        @pl.when(head == last)
        def _():
            send_last(total, 1)

        @pl.when(head > 0)
        def _():
            finish(head - 1)

        @pl.when(head == 0)
        def _():
            advance_o(3, 1)

        @pl.when(head == max(last - 2, 0))
        def _():
            complete_o(range(2))

        @pl.when(head == max(last - 1, 0))
        def _():
            complete_o(range(2, CHUNKS))

        @pl.when(head < last)
        def _():
            for part in range(2):
                core_copy(head, part).wait_send()
            wait_sent(head)

    for d in red_steps:
        reduced_copy(d).wait_send()
    if passing:
        for d in red_steps:
            pass_copy(d).wait_send()
    for d in ctx_steps:
        delta_copy(d).wait_send()
    for chunk in range(CHUNKS):
        for stage in range(bits):
            stage_copy(group_o(chunk), stage).wait_send()
    for part in range(2):
        core_copy(last, part).wait_send()
    wait_sent(last)

    for chunk in range(CHUNKS):
        at = slice(chunk * part_width, (chunk + 1) * part_width)
        total = final_own_o[chunk, me]
        for d in ctx_steps:
            final_copy_o(chunk, d).wait()
            total += final_in_o[chunk, d - 1].astype(WIDE)
        out_ref[3, :, at] = total

    for head in range(last):
        for d in range(1, fars):
            far_copy(head, d).wait_send()
        for d in range(ctx_size):
            if d:
                final_copy(head, d).wait()
                block = final_in[head, d - 1].astype(WIDE)
            else:
                block = final_own[head, me]
            for index in range(3):
                span = slice(index * width, (index + 1) * width)
                out_ref[index, :, columns(me ^ d, head)] = block[:, span]

    for part, own, arrived, first in ((0, last_own_v, last_in_v, 2), (1, last_own_qk, last_in_qk, 0)):
        wait_last(part)
        for d in range(ctx_size):
            total = None if d else own[far, me]
            for f in range(fars):
                if f or d:
                    block = arrived[f * ctx_size + d].astype(WIDE)
                    total = block if total is None else total + block
            for index in range(own.shape[3] // width):
                span = slice(index * width, (index + 1) * width)
                out_ref[first + index, :, columns(me ^ d, last)] = total[:, span]


def on_device(
    dp_size,
    ctx_size,
    layer_input,
    queries,
    key_rows,
    value_rows,
    attn_out,
    out_grad,
    layer_grad,
    logsum,
    projector,
):
    rows, features = queries.shape[1:]
    all_heads, tokens = logsum.shape[1:]
    heads = all_heads // ctx_size
    width = features // all_heads
    depth, rank = projector.shape
    bits = dp_size.bit_length() - 1
    fars = dp_size // 2
    piece = rank // dp_size
    slab = piece // ctx_size
    padded = -(-heads // 8) * 8
    half = rank // 2
    both = 2 * width
    three = 3 * width
    part_width = features // CHUNKS
    others = ctx_size - 1
    dma = pltpu.SemaphoreType.DMA
    anywhere = pl.BlockSpec(memory_space=pl.ANY)
    in_vmem = pl.BlockSpec(memory_space=pltpu.VMEM)
    return pl.pallas_call(
        functools.partial(kernel, dp_size, ctx_size),
        out_shape=pltpu.VMEM((4, slab, features), WIDE),
        in_specs=[anywhere] * 7 + [in_vmem, anywhere],
        out_specs=in_vmem,
        scratch_shapes=[
            pltpu.VMEM((4, heads, tokens, width), LOW),
            pltpu.VMEM((2 * rows, depth), LOW),
            pltpu.VMEM((depth, rank), LOW),
            pltpu.VMEM((2 * rows, rank), WIDE),
            pltpu.VMEM((rows, features), LOW),
            pltpu.VMEM((rows, features), LOW),
            pltpu.VMEM((tokens, rank), LOW),
            pltpu.VMEM((2, half, tokens), LOW),
            pltpu.VMEM((rows, rank), LOW),
            pltpu.VMEM((ctx_size, padded, rows), WIDE),
            pltpu.VMEM((ctx_size, padded, rows), WIDE),
            pltpu.VMEM((padded, tokens), WIDE),
            pltpu.VMEM((tokens, tokens), WIDE),
            pltpu.VMEM((tokens, width), WIDE),
            pltpu.VMEM((tokens, width), LOW),
            pltpu.VMEM((tokens, both), LOW),
            pltpu.VMEM((half, width), WIDE),
            pltpu.VMEM((heads, half, width), LOW),
            pltpu.VMEM((heads, half, width), LOW),
            pltpu.VMEM((heads, half, both), LOW),
            pltpu.VMEM((heads, half, both), LOW),
            pltpu.VMEM((heads, fars, piece, three), WIDE),
            pltpu.VMEM((heads, fars, piece, three), LOW),
            pltpu.VMEM((heads, fars - 1, piece, three), LOW),
            pltpu.VMEM((heads, ctx_size, slab, three), WIDE),
            pltpu.VMEM((heads, ctx_size, slab, three), LOW),
            pltpu.VMEM((heads, others, slab, three), LOW),
            pltpu.VMEM((fars, ctx_size, slab, width), WIDE),
            pltpu.VMEM((fars * ctx_size, slab, width), LOW),
            pltpu.VMEM((fars * ctx_size, slab, width), LOW),
            pltpu.VMEM((fars, ctx_size, slab, both), WIDE),
            pltpu.VMEM((fars * ctx_size, slab, both), LOW),
            pltpu.VMEM((fars * ctx_size, slab, both), LOW),
            pltpu.VMEM((CHUNKS, dp_size, piece, part_width), WIDE),
            pltpu.VMEM((CHUNKS, dp_size - 1, piece, part_width), LOW),
            pltpu.VMEM((CHUNKS, dp_size - 1, piece, part_width), LOW),
            pltpu.VMEM((CHUNKS, ctx_size, slab, part_width), WIDE),
            pltpu.VMEM((CHUNKS, ctx_size, slab, part_width), LOW),
            pltpu.VMEM((CHUNKS, others, slab, part_width), LOW),
            dma((5,)),
            dma((heads, 4)),
            dma((heads, 4, others)),
            dma((heads, 4, others)),
            dma((others,)),
            dma((others,)),
            dma((2,)),
            dma((2,)),
            dma((others,)),
            dma((others,)),
            dma((heads, 2)),
            dma((heads, 2)),
            dma((heads, fars - 1)),
            dma((heads, fars - 1)),
            dma((heads, others)),
            dma((heads, others)),
            dma((2,)),
            dma((2,)),
            dma((CHUNKS, bits)),
            dma((CHUNKS, bits)),
            dma((CHUNKS, others)),
            dma((CHUNKS, others)),
            pltpu.SemaphoreType.REGULAR((2,)),
        ],
        compiler_params=pltpu.CompilerParams(
            collective_id=0, has_side_effects=True, vmem_limit_bytes=56 * 1024 * 1024
        ),
    )(
        layer_input[0],
        queries[0],
        key_rows[0],
        value_rows[0],
        attn_out[0],
        out_grad[0],
        layer_grad[0],
        logsum[0],
        projector,
    )


def solution(mesh):
    rows = P("dp", "ctx", None)
    placed = (rows,) * 7 + (P("dp", None, None), P())
    return jax.shard_map(
        functools.partial(on_device, mesh.shape["dp"], mesh.shape["ctx"]),
        mesh=mesh,
        in_specs=placed,
        out_specs=P(None, ("dp", "ctx"), None),
        check_vma=False,
    )
```

```python
import functools
import math

import jax
import jax.numpy as jnp
from jax import lax
from jax.experimental import pallas as pl
from jax.experimental.pallas import tpu as pltpu
from jax.sharding import PartitionSpec as P

BLOCK = 128
DEPTH = 512
CHUNKS = 4
MESH = pl.DeviceIdType.MESH
LOW, WIDE = jnp.bfloat16, jnp.float32


def dot(left, right, dims):
    return lax.dot_general(left, right, (dims, ((), ())), preferred_element_type=jnp.float32)


def value_products(arrays, head, sums, prob_ref, dv_low):
    q_ref, k_ref, g_ref = (arrays.at[index, head] for index in range(3))
    tokens, width = q_ref.shape
    scaling = 1.0 / math.sqrt(width)
    row = lax.broadcasted_iota(jnp.int32, (BLOCK, BLOCK), 0)
    col = lax.broadcasted_iota(jnp.int32, (BLOCK, BLOCK), 1)
    causal = row <= col
    for start in range(0, tokens, BLOCK):
        span = slice(start, start + BLOCK)
        scores = dot(k_ref[span], q_ref[start:], ((1,), (1,))) * scaling
        prob = jnp.exp(scores - sums[:, start:])
        diagonal = jnp.where(causal, prob[:, :BLOCK], 0.0)
        if start + BLOCK < tokens:
            prob = jnp.concatenate([diagonal, prob[:, BLOCK:]], axis=1)
        else:
            prob = diagonal
        prob_ref[span, start:] = prob
        dv_low[span] = dot(prob.astype(LOW), g_ref[start:], ((1,), (0,))).astype(LOW)


def score_products(arrays, head, deltas, prob_ref, acc, qk_low, between):
    q_ref, k_ref, g_ref, v_ref = (arrays.at[index, head] for index in range(4))
    tokens, width = q_ref.shape
    scaling = 1.0 / math.sqrt(width)
    for start in range(0, tokens, BLOCK):
        span = slice(start, start + BLOCK)
        dprob = dot(v_ref[span], g_ref[start:], ((1,), (1,)))
        dscore = prob_ref[span, start:] * (dprob - deltas[:, start:]) * scaling
        score_low = dscore.astype(LOW)
        dquery = dot(score_low, k_ref[span], ((0,), (0,)))
        if start == 0:
            acc[...] = dquery
        else:
            acc[start:] += dquery
        qk_low[span, :width] = acc[span].astype(LOW)
        qk_low[span, width:] = dot(score_low, q_ref[start:], ((1,), (0,))).astype(LOW)
        if start == BLOCK:
            between()


def kernel(
    dp_size,
    ctx_size,
    layer_input,
    q_hbm,
    k_hbm,
    v_hbm,
    o_hbm,
    g_hbm,
    layer_grad,
    sums_ref,
    projector,
    out_ref,
    arrays,
    rows_in,
    proj,
    proj_acc,
    grad_own,
    out_own,
    reduced,
    reduced_t,
    reduced_grad,
    delta_out,
    delta_in,
    delta_rows,
    prob_ref,
    acc,
    dv_low,
    qk_low,
    mine_v,
    core_out_v,
    core_in_v,
    core_out_qk,
    core_in_qk,
    total_ref,
    far_out,
    far_in,
    final_own,
    final_out,
    final_in,
    last_own_v,
    last_out_v,
    last_in_v,
    last_own_qk,
    last_out_qk,
    last_in_qk,
    own_o,
    sum_out_o,
    sum_in_o,
    final_own_o,
    final_out_o,
    final_in_o,
    load_sem,
    local_sem,
    head_send,
    head_recv,
    red_send,
    red_recv,
    pass_send,
    pass_recv,
    delta_send,
    delta_recv,
    core_send,
    core_recv,
    far_send,
    far_recv,
    final_send,
    final_recv,
    last_send,
    last_recv,
    sum_send_o,
    sum_recv_o,
    final_send_o,
    final_recv_o,
    known,
):
    me = lax.axis_index("ctx")
    place = lax.axis_index("dp")
    bits = dp_size.bit_length() - 1
    fars = dp_size // 2
    core = lax.rem(place, 2)
    far = place // 2
    sources = (q_hbm, k_hbm, g_hbm, v_hbm)
    count = len(sources)
    heads = arrays.shape[1]
    last = heads - 1
    rows = q_hbm.shape[0]
    width = arrays.shape[3]
    depth = projector.shape[0]
    rank = projector.shape[1]
    piece = rank // dp_size
    slab = piece // ctx_size
    both = 2 * width
    passing = ctx_size == 4
    near = ctx_size == 4 and fars == 4
    mine = pl.ds(pl.multiple_of(me * rows, 16), rows)
    ctx_steps = range(1, ctx_size)

    def columns(owner, head):
        return pl.ds(pl.multiple_of((owner * heads + head) * width, width), width)

    def remote(src, dst, send, recv, **where):
        return pltpu.make_async_remote_copy(
            src_ref=src,
            dst_ref=dst,
            send_sem=send,
            recv_sem=recv,
            device_id=where,
            device_id_type=MESH,
        )

    def local_copy(head, index):
        return pltpu.make_async_copy(
            sources[index].at[:, columns(me, head)],
            arrays.at[index, head, mine],
            local_sem.at[head, index],
        )

    def head_copy(head, index, d):
        peer = me ^ d
        return remote(
            sources[index].at[:, columns(peer, head)],
            arrays.at[index, head, mine],
            head_send.at[head, index, d - 1],
            head_recv.at[head, index, d - 1],
            ctx=peer,
        )

    def start_head(head, indices):
        for index in indices:
            for d in ctx_steps:
                head_copy(head, index, d).start()
        for index in indices:
            local_copy(head, index).start()

    def wait_sent(head):
        for index in range(count):
            for d in ctx_steps:
                head_copy(head, index, d).wait_send()

    def wait_head(head, indices):
        for index in indices:
            local_copy(head, index).wait()
            for d in ctx_steps:
                head_copy(head, index, d).wait_recv()

    red_steps = (1, 2) if passing else tuple(ctx_steps)

    def reduced_copy(d):
        return remote(
            reduced.at[mine],
            reduced.at[mine],
            red_send.at[d - 1],
            red_recv.at[d - 1],
            ctx=me ^ d,
        )

    def pass_copy(d):
        half = rows // 2
        at = pl.ds(pl.multiple_of((me ^ d) * rows + (d - 1) * half, 16), half)
        return remote(
            reduced.at[at],
            reduced.at[at],
            pass_send.at[d - 1],
            pass_recv.at[d - 1],
            ctx=me ^ (3 - d),
        )

    def delta_copy(d):
        peer = me ^ d
        return remote(
            delta_out.at[peer],
            delta_in.at[me],
            delta_send.at[d - 1],
            delta_recv.at[d - 1],
            ctx=peer,
        )

    def core_copy(head, part):
        out, arrived = ((core_out_v, core_in_v), (core_out_qk, core_in_qk))[part]
        return remote(
            out.at[head],
            arrived.at[head],
            core_send.at[head, part],
            core_recv.at[head, part],
            dp=place ^ 1,
        )

    def far_copy(head, d):
        return remote(
            far_out.at[head, far ^ d],
            far_in.at[head, d - 1],
            far_send.at[head, d - 1],
            far_recv.at[head, d - 1],
            dp=place ^ (2 * d),
        )

    def final_copy(head, d):
        peer = me ^ d
        return remote(
            final_out.at[head, peer],
            final_in.at[head, d - 1],
            final_send.at[head, d - 1],
            final_recv.at[head, d - 1],
            ctx=peer,
        )

    def last_copy(part, f, d):
        out, arrived = ((last_out_v, last_in_v), (last_out_qk, last_in_qk))[part]
        return remote(
            out.at[(far ^ f) * ctx_size + (me ^ d)],
            arrived.at[f * ctx_size + d],
            last_send.at[part],
            last_recv.at[part],
            dp=place ^ (2 * f),
            ctx=me ^ d,
        )

    def wait_last(part):
        arrived = (last_in_v, last_in_qk)[part]
        all_others = arrived.at[pl.ds(1, fars * ctx_size - 1)]
        for sem in (last_recv, last_send):
            pltpu.make_async_copy(all_others, all_others, sem.at[part]).wait()

    last_steps = [
        (f, d) for f in reversed(range(fars)) for d in reversed(range(ctx_size)) if f or d
    ]

    def group_o(chunk):
        return tuple(ref.at[chunk] for ref in (own_o, sum_out_o, sum_in_o, sum_send_o, sum_recv_o))

    def place_bit(stage):
        return lax.rem(place // 2**stage, 2)

    def stage_copy(group, stage):
        half = dp_size // 2 ** (stage + 1)
        span = pl.ds(dp_size - 2 * half, half)
        return remote(
            group[1].at[span],
            group[2].at[span],
            group[3].at[stage],
            group[4].at[stage],
            dp=place ^ 2**stage,
        )

    def stage_blocks(stage, bit):
        half = dp_size // 2 ** (stage + 1)
        first = lax.rem(place, 2**stage) + bit * 2**stage
        return [(first + 2 ** (stage + 1) * j, dp_size - 2 * half + j) for j in range(half)]

    def send_stage(group, stage):
        for block, slot in stage_blocks(stage, 1 - place_bit(stage)):
            group[1][slot] = group[0][block].astype(LOW)
        stage_copy(group, stage).start()

    def add_stage(group, stage):
        stage_copy(group, stage).wait_recv()
        for block, slot in stage_blocks(stage, place_bit(stage)):
            group[0][block] += group[2][slot].astype(WIDE)

    def final_copy_o(chunk, d):
        peer = me ^ d
        return remote(
            final_out_o.at[chunk, peer],
            final_in_o.at[chunk, d - 1],
            final_send_o.at[chunk, d - 1],
            final_recv_o.at[chunk, d - 1],
            ctx=peer,
        )

    def advance_o(chunk, stage):
        group = group_o(chunk)
        add_stage(group, stage)
        if stage + 1 < bits:
            send_stage(group, stage + 1)
            return
        total = own_o[chunk, place]
        for to in range(ctx_size):
            part = total[to * slab : (to + 1) * slab]
            final_own_o[chunk, to] = part
            final_out_o[chunk, to] = part.astype(LOW)
        for d in ctx_steps:
            final_copy_o(chunk, d).start()

    loads = (
        pltpu.make_async_copy(projector, proj, load_sem.at[0]),
        pltpu.make_async_copy(layer_input, rows_in.at[:rows], load_sem.at[1]),
        pltpu.make_async_copy(layer_grad, rows_in.at[rows:], load_sem.at[2]),
        pltpu.make_async_copy(o_hbm, out_own, load_sem.at[3]),
        pltpu.make_async_copy(g_hbm, grad_own, load_sem.at[4]),
    )
    barrier = pltpu.get_barrier_semaphore()
    greet_ctx = (1, 2) if near else tuple(ctx_steps)
    greet_dp = (0,) if near else tuple(range(bits))
    for d in greet_ctx:
        pl.semaphore_signal(barrier, inc=1, device_id={"ctx": me ^ d}, device_id_type=MESH)
    for stage in greet_dp:
        peer = place ^ 2**stage
        pl.semaphore_signal(barrier, inc=1, device_id={"dp": peer}, device_id_type=MESH)
    if near:

        @pl.when(far > 0)
        def _():
            pl.semaphore_signal(barrier, inc=1, device_id={"dp": place - 2}, device_id_type=MESH)

        @pl.when(far < fars - 1)
        def _():
            pl.semaphore_signal(barrier, inc=1, device_id={"dp": place + 2}, device_id_type=MESH)

    for load in loads:
        load.start()
    greeted = len(greet_ctx) + len(greet_dp)
    if near:
        inner = jnp.logical_and(far > 0, far < fars - 1)
        pl.semaphore_wait(barrier, greeted + 1 + inner.astype(jnp.int32))
        for index in range(2):
            for d in (1, 2):
                head_copy(0, index, d).start()
        pl.semaphore_signal(known.at[0], inc=1, device_id={"ctx": me ^ 1}, device_id_type=MESH)

        @pl.when(inner)
        def _():
            for step in (-2, 2):
                pl.semaphore_signal(
                    known.at[1], inc=1, device_id={"dp": place + step}, device_id_type=MESH
                )

        pl.semaphore_wait(known.at[0], 1)
        for index in range(2):
            head_copy(0, index, 3).start()
            local_copy(0, index).start()
    else:
        pl.semaphore_wait(barrier, greeted)
        start_head(0, range(2))
    for load in loads[:3]:
        load.wait()
    proj_acc[...] = jnp.zeros_like(proj_acc)

    @pl.loop(0, depth // DEPTH)
    def _(step):
        at = pl.ds(pl.multiple_of(step * DEPTH, DEPTH), DEPTH)
        proj_acc[...] += dot(rows_in[:, at], proj[at], ((1,), (0,)))

    reduced[mine] = proj_acc[:rows].astype(LOW)
    for d in red_steps:
        reduced_copy(d).start()
    start_head(0, range(2, count))
    reduced_grad[...] = proj_acc[rows:].astype(LOW)
    for load in loads[3:]:
        load.wait()
    rgrad_t = reduced_grad[...].T
    part_width = own_o.shape[3]
    for chunk in range(CHUNKS):
        at = slice(chunk * part_width, (chunk + 1) * part_width)
        for part in range(dp_size):
            span = slice(part * piece, (part + 1) * piece)
            own_o[chunk, part] = dot(rgrad_t[span], out_own[:, at], ((1,), (0,)))
        send_stage(group_o(chunk), 0)

    lane = lax.broadcasted_iota(jnp.int32, (rows, BLOCK), 1)
    table = jnp.zeros((rows, BLOCK), WIDE)
    for head in range(heads * ctx_size):
        span = slice(head * width, (head + 1) * width)
        product = grad_own[:, span].astype(WIDE) * out_own[:, span].astype(WIDE)
        table = jnp.where(lane == head, jnp.sum(product, axis=1, keepdims=True), table)
    table = table.T
    delta_out[...] = jnp.zeros_like(delta_out)
    for owner in range(ctx_size):
        delta_out[owner, :heads] = table[owner * heads : (owner + 1) * heads]
    delta_in[me] = delta_out[me]
    for d in ctx_steps:
        delta_copy(d).start()
    if near:
        pl.semaphore_wait(known.at[1], 1)
    for chunk in range(2):
        advance_o(chunk, 0)

    def complete_o(chunks):
        for chunk in chunks:
            for stage in range(2, bits):
                advance_o(chunk, stage)

    for d in red_steps:
        reduced_copy(d).wait_recv()
        if passing:
            pass_copy(d).start()
    for head in range(1, heads):
        start_head(head, range(count))
    advance_o(0, 1)
    advance_o(2, 0)

    def gather_reduced():
        advance_o(1, 1)
        advance_o(3, 0)
        for d in ctx_steps:
            delta_copy(d).wait_recv()
        delta_rows[...] = jnp.concatenate([delta_in[owner] for owner in range(ctx_size)], axis=1)
        if passing:
            for d in red_steps:
                pass_copy(d).wait_recv()
        turned = reduced[...].T
        for part in range(dp_size):
            block = turned[part * piece : (part + 1) * piece]
            reduced_t[part % 2, (part // 2) * piece : (part // 2 + 1) * piece] = block

    def keep(head, total, lanes):
        for f in range(fars):
            block = total[f * piece : (f + 1) * piece]
            total_ref[head, f, :, lanes] = block
            far_out[head, f, :, lanes] = block.astype(LOW)

    def send_last(total, part):
        own, out = ((last_own_v, last_out_v), (last_own_qk, last_out_qk))[part]
        for f in range(fars):
            for to in range(ctx_size):
                first = f * piece + to * slab
                block = total[first : first + slab]
                own[f, to] = block
                out[f * ctx_size + to] = block.astype(LOW)
        for f, d in last_steps:
            last_copy(part, f, d).start()

    def finish(head):
        total = total_ref[head, far]
        for d in range(1, fars):
            far_copy(head, d).wait_recv()
            total += far_in[head, d - 1].astype(WIDE)
        for to in range(ctx_size):
            block = total[to * slab : (to + 1) * slab]
            final_own[head, to] = block
            final_out[head, to] = block.astype(LOW)
        for d in ctx_steps:
            final_copy(head, d).start()

    @pl.loop(0, heads)
    def _(head):
        wait_head(head, range(3))
        sums = sums_ref[pl.ds(me * heads + head, 1), :]
        value_products(arrays, head, sums, prob_ref, dv_low)

        @pl.when(head == 0)
        def _():
            gather_reduced()

        @pl.when(head == 1)
        def _():
            advance_o(3, 1)

        low = dv_low[...]
        core_out_v[head] = dot(reduced_t[1 - core], low, ((1,), (0,))).astype(LOW)
        core_copy(head, 0).start()
        mine_v[...] = dot(reduced_t[core], low, ((1,), (0,)))

        def add_values():
            core_copy(head, 0).wait_recv()
            total = mine_v[...] + core_in_v[head].astype(WIDE)

            @pl.when(head < last)
            def _():
                keep(head, total, slice(both, both + width))

            @pl.when(head == last)
            def _():
                send_last(total, 0)

        wait_head(head, range(3, count))
        deltas = delta_rows[pl.ds(head, 1), :]
        score_products(arrays, head, deltas, prob_ref, acc, qk_low, add_values)
        low = qk_low[...]
        core_out_qk[head] = dot(reduced_t[1 - core], low, ((1,), (0,))).astype(LOW)
        core_copy(head, 1).start()
        joined = dot(reduced_t[core], low, ((1,), (0,)))
        core_copy(head, 1).wait_recv()
        total = joined + core_in_qk[head].astype(WIDE)

        @pl.when(head < last)
        def _():
            keep(head, total, slice(0, both))
            for d in reversed(range(1, fars)):
                far_copy(head, d).start()

        @pl.when(head == last)
        def _():
            send_last(total, 1)

        @pl.when(head == 0)
        def _():
            advance_o(2, 1)

        @pl.when(head == max(last - 2, 0))
        def _():
            complete_o(range(2))

        @pl.when(head == max(last - 1, 1))
        def _():
            complete_o(range(2, CHUNKS))

        @pl.when(head < last)
        def _():
            for part in range(2):
                core_copy(head, part).wait_send()
            wait_sent(head)

    for d in red_steps:
        reduced_copy(d).wait_send()
    if passing:
        for d in red_steps:
            pass_copy(d).wait_send()
    for d in ctx_steps:
        delta_copy(d).wait_send()
    for chunk in range(CHUNKS):
        for stage in range(bits):
            stage_copy(group_o(chunk), stage).wait_send()
    for head in range(last):
        finish(head)
    for part in range(2):
        core_copy(last, part).wait_send()
    wait_sent(last)

    for chunk in range(CHUNKS):
        at = slice(chunk * part_width, (chunk + 1) * part_width)
        total = final_own_o[chunk, me]
        for d in ctx_steps:
            final_copy_o(chunk, d).wait()
            total += final_in_o[chunk, d - 1].astype(WIDE)
        out_ref[3, :, at] = total

    for head in range(last):
        for d in range(1, fars):
            far_copy(head, d).wait_send()
        for d in range(ctx_size):
            if d:
                final_copy(head, d).wait()
                block = final_in[head, d - 1].astype(WIDE)
            else:
                block = final_own[head, me]
            for index in range(3):
                span = slice(index * width, (index + 1) * width)
                out_ref[index, :, columns(me ^ d, head)] = block[:, span]

    for part, own, arrived, first in ((0, last_own_v, last_in_v, 2), (1, last_own_qk, last_in_qk, 0)):
        wait_last(part)
        for d in range(ctx_size):
            total = None if d else own[far, me]
            for f in range(fars):
                if f or d:
                    block = arrived[f * ctx_size + d].astype(WIDE)
                    total = block if total is None else total + block
            for index in range(own.shape[3] // width):
                span = slice(index * width, (index + 1) * width)
                out_ref[first + index, :, columns(me ^ d, last)] = total[:, span]


def on_device(
    dp_size,
    ctx_size,
    layer_input,
    queries,
    key_rows,
    value_rows,
    attn_out,
    out_grad,
    layer_grad,
    logsum,
    projector,
):
    rows, features = queries.shape[1:]
    all_heads, tokens = logsum.shape[1:]
    heads = all_heads // ctx_size
    width = features // all_heads
    depth, rank = projector.shape
    bits = dp_size.bit_length() - 1
    fars = dp_size // 2
    piece = rank // dp_size
    slab = piece // ctx_size
    padded = -(-heads // 8) * 8
    half = rank // 2
    both = 2 * width
    three = 3 * width
    part_width = features // CHUNKS
    others = ctx_size - 1
    dma = pltpu.SemaphoreType.DMA
    anywhere = pl.BlockSpec(memory_space=pl.ANY)
    in_vmem = pl.BlockSpec(memory_space=pltpu.VMEM)
    return pl.pallas_call(
        functools.partial(kernel, dp_size, ctx_size),
        out_shape=pltpu.VMEM((4, slab, features), WIDE),
        in_specs=[anywhere] * 7 + [in_vmem, anywhere],
        out_specs=in_vmem,
        scratch_shapes=[
            pltpu.VMEM((4, heads, tokens, width), LOW),
            pltpu.VMEM((2 * rows, depth), LOW),
            pltpu.VMEM((depth, rank), LOW),
            pltpu.VMEM((2 * rows, rank), WIDE),
            pltpu.VMEM((rows, features), LOW),
            pltpu.VMEM((rows, features), LOW),
            pltpu.VMEM((tokens, rank), LOW),
            pltpu.VMEM((2, half, tokens), LOW),
            pltpu.VMEM((rows, rank), LOW),
            pltpu.VMEM((ctx_size, padded, rows), WIDE),
            pltpu.VMEM((ctx_size, padded, rows), WIDE),
            pltpu.VMEM((padded, tokens), WIDE),
            pltpu.VMEM((tokens, tokens), WIDE),
            pltpu.VMEM((tokens, width), WIDE),
            pltpu.VMEM((tokens, width), LOW),
            pltpu.VMEM((tokens, both), LOW),
            pltpu.VMEM((half, width), WIDE),
            pltpu.VMEM((heads, half, width), LOW),
            pltpu.VMEM((heads, half, width), LOW),
            pltpu.VMEM((heads, half, both), LOW),
            pltpu.VMEM((heads, half, both), LOW),
            pltpu.VMEM((heads, fars, piece, three), WIDE),
            pltpu.VMEM((heads, fars, piece, three), LOW),
            pltpu.VMEM((heads, fars - 1, piece, three), LOW),
            pltpu.VMEM((heads, ctx_size, slab, three), WIDE),
            pltpu.VMEM((heads, ctx_size, slab, three), LOW),
            pltpu.VMEM((heads, others, slab, three), LOW),
            pltpu.VMEM((fars, ctx_size, slab, width), WIDE),
            pltpu.VMEM((fars * ctx_size, slab, width), LOW),
            pltpu.VMEM((fars * ctx_size, slab, width), LOW),
            pltpu.VMEM((fars, ctx_size, slab, both), WIDE),
            pltpu.VMEM((fars * ctx_size, slab, both), LOW),
            pltpu.VMEM((fars * ctx_size, slab, both), LOW),
            pltpu.VMEM((CHUNKS, dp_size, piece, part_width), WIDE),
            pltpu.VMEM((CHUNKS, dp_size - 1, piece, part_width), LOW),
            pltpu.VMEM((CHUNKS, dp_size - 1, piece, part_width), LOW),
            pltpu.VMEM((CHUNKS, ctx_size, slab, part_width), WIDE),
            pltpu.VMEM((CHUNKS, ctx_size, slab, part_width), LOW),
            pltpu.VMEM((CHUNKS, others, slab, part_width), LOW),
            dma((5,)),
            dma((heads, 4)),
            dma((heads, 4, others)),
            dma((heads, 4, others)),
            dma((others,)),
            dma((others,)),
            dma((2,)),
            dma((2,)),
            dma((others,)),
            dma((others,)),
            dma((heads, 2)),
            dma((heads, 2)),
            dma((heads, fars - 1)),
            dma((heads, fars - 1)),
            dma((heads, others)),
            dma((heads, others)),
            dma((2,)),
            dma((2,)),
            dma((CHUNKS, bits)),
            dma((CHUNKS, bits)),
            dma((CHUNKS, others)),
            dma((CHUNKS, others)),
            pltpu.SemaphoreType.REGULAR((2,)),
        ],
        compiler_params=pltpu.CompilerParams(
            collective_id=0, has_side_effects=True, vmem_limit_bytes=56 * 1024 * 1024
        ),
    )(
        layer_input[0],
        queries[0],
        key_rows[0],
        value_rows[0],
        attn_out[0],
        out_grad[0],
        layer_grad[0],
        logsum[0],
        projector,
    )


def solution(mesh):
    rows = P("dp", "ctx", None)
    placed = (rows,) * 7 + (P("dp", None, None), P())
    return jax.shard_map(
        functools.partial(on_device, mesh.shape["dp"], mesh.shape["ctx"]),
        mesh=mesh,
        in_specs=placed,
        out_specs=P(None, ("dp", "ctx"), None),
        check_vma=False,
    )
```

```python
import functools
import math

import jax
import jax.numpy as jnp
from jax import lax
from jax.experimental import pallas as pl
from jax.experimental.pallas import tpu as pltpu
from jax.sharding import PartitionSpec as P

BLOCK = 128
DEPTH = 512
CHUNKS = 4
MESH = pl.DeviceIdType.MESH
LOW, WIDE = jnp.bfloat16, jnp.float32


def dot(left, right, dims):
    return lax.dot_general(left, right, (dims, ((), ())), preferred_element_type=jnp.float32)


def value_products(arrays, head, sums, prob_ref, dv_low):
    q_ref, k_ref, g_ref = (arrays.at[index, head] for index in range(3))
    tokens, width = q_ref.shape
    scaling = 1.0 / math.sqrt(width)
    row = lax.broadcasted_iota(jnp.int32, (BLOCK, BLOCK), 0)
    col = lax.broadcasted_iota(jnp.int32, (BLOCK, BLOCK), 1)
    causal = row <= col
    for start in range(0, tokens, BLOCK):
        span = slice(start, start + BLOCK)
        scores = dot(k_ref[span], q_ref[start:], ((1,), (1,))) * scaling
        prob = jnp.exp(scores - sums[:, start:])
        diagonal = jnp.where(causal, prob[:, :BLOCK], 0.0)
        if start + BLOCK < tokens:
            prob = jnp.concatenate([diagonal, prob[:, BLOCK:]], axis=1)
        else:
            prob = diagonal
        prob_ref[span, start:] = prob
        dv_low[span] = dot(prob.astype(LOW), g_ref[start:], ((1,), (0,))).astype(LOW)


def score_products(arrays, head, deltas, prob_ref, acc, qk_low, between):
    q_ref, k_ref, g_ref, v_ref = (arrays.at[index, head] for index in range(4))
    tokens, width = q_ref.shape
    scaling = 1.0 / math.sqrt(width)
    for start in range(0, tokens, BLOCK):
        span = slice(start, start + BLOCK)
        dprob = dot(v_ref[span], g_ref[start:], ((1,), (1,)))
        dscore = prob_ref[span, start:] * (dprob - deltas[:, start:]) * scaling
        score_low = dscore.astype(LOW)
        dquery = dot(score_low, k_ref[span], ((0,), (0,)))
        if start == 0:
            acc[...] = dquery
        else:
            acc[start:] += dquery
        qk_low[span, :width] = acc[span].astype(LOW)
        qk_low[span, width:] = dot(score_low, q_ref[start:], ((1,), (0,))).astype(LOW)
        if start == BLOCK:
            between()


def kernel(
    dp_size,
    ctx_size,
    layer_input,
    q_hbm,
    k_hbm,
    v_hbm,
    o_hbm,
    g_hbm,
    layer_grad,
    sums_ref,
    projector,
    out_ref,
    arrays,
    rows_in,
    proj,
    proj_acc,
    grad_own,
    out_own,
    reduced,
    reduced_t,
    reduced_grad,
    delta_out,
    delta_in,
    delta_rows,
    prob_ref,
    acc,
    dv_low,
    qk_low,
    mine_v,
    core_out_v,
    core_in_v,
    core_out_qk,
    core_in_qk,
    total_ref,
    far_out,
    far_in,
    final_own,
    final_out,
    final_in,
    last_own_v,
    last_out_v,
    last_in_v,
    last_own_qk,
    last_out_qk,
    last_in_qk,
    own_o,
    sum_out_o,
    sum_in_o,
    final_own_o,
    final_out_o,
    final_in_o,
    load_sem,
    local_sem,
    head_send,
    head_recv,
    red_send,
    red_recv,
    pass_send,
    pass_recv,
    delta_send,
    delta_recv,
    core_send,
    core_recv,
    far_send,
    far_recv,
    final_send,
    final_recv,
    last_send,
    last_recv,
    sum_send_o,
    sum_recv_o,
    final_send_o,
    final_recv_o,
    known,
):
    me = lax.axis_index("ctx")
    place = lax.axis_index("dp")
    bits = dp_size.bit_length() - 1
    fars = dp_size // 2
    core = lax.rem(place, 2)
    far = place // 2
    sources = (q_hbm, k_hbm, g_hbm, v_hbm)
    count = len(sources)
    heads = arrays.shape[1]
    last = heads - 1
    rows = q_hbm.shape[0]
    width = arrays.shape[3]
    depth = projector.shape[0]
    rank = projector.shape[1]
    piece = rank // dp_size
    slab = piece // ctx_size
    both = 2 * width
    passing = ctx_size == 4
    near = ctx_size == 4 and fars == 4
    mine = pl.ds(pl.multiple_of(me * rows, 16), rows)
    ctx_steps = range(1, ctx_size)

    def columns(owner, head):
        return pl.ds(pl.multiple_of((owner * heads + head) * width, width), width)

    def remote(src, dst, send, recv, **where):
        return pltpu.make_async_remote_copy(
            src_ref=src,
            dst_ref=dst,
            send_sem=send,
            recv_sem=recv,
            device_id=where,
            device_id_type=MESH,
        )

    def local_copy(head, index):
        return pltpu.make_async_copy(
            sources[index].at[:, columns(me, head)],
            arrays.at[index, head, mine],
            local_sem.at[head, index],
        )

    def head_copy(head, index, d):
        peer = me ^ d
        return remote(
            sources[index].at[:, columns(peer, head)],
            arrays.at[index, head, mine],
            head_send.at[head, index, d - 1],
            head_recv.at[head, index, d - 1],
            ctx=peer,
        )

    def start_head(head, indices):
        for index in indices:
            for d in reversed(ctx_steps):
                head_copy(head, index, d).start()
        for index in indices:
            local_copy(head, index).start()

    def wait_sent(head):
        for index in range(count):
            for d in ctx_steps:
                head_copy(head, index, d).wait_send()

    def wait_head(head, indices):
        for index in indices:
            local_copy(head, index).wait()
            for d in ctx_steps:
                head_copy(head, index, d).wait_recv()

    red_steps = (1, 2) if passing else tuple(ctx_steps)

    def reduced_copy(d):
        return remote(
            reduced.at[mine],
            reduced.at[mine],
            red_send.at[d - 1],
            red_recv.at[d - 1],
            ctx=me ^ d,
        )

    def pass_copy(d):
        half = rows // 2
        at = pl.ds(pl.multiple_of((me ^ d) * rows + (d - 1) * half, 16), half)
        return remote(
            reduced.at[at],
            reduced.at[at],
            pass_send.at[d - 1],
            pass_recv.at[d - 1],
            ctx=me ^ (3 - d),
        )

    def delta_copy(d):
        peer = me ^ d
        return remote(
            delta_out.at[peer],
            delta_in.at[me],
            delta_send.at[d - 1],
            delta_recv.at[d - 1],
            ctx=peer,
        )

    def core_copy(head, part):
        out, arrived = ((core_out_v, core_in_v), (core_out_qk, core_in_qk))[part]
        return remote(
            out.at[head],
            arrived.at[head],
            core_send.at[head, part],
            core_recv.at[head, part],
            dp=place ^ 1,
        )

    def far_copy(head, part, d):
        lanes = (pl.ds(both, width), pl.ds(0, both))[part]
        return remote(
            far_out.at[head, far ^ d, :, lanes],
            far_in.at[head, d - 1, :, lanes],
            far_send.at[head, part, d - 1],
            far_recv.at[head, part, d - 1],
            dp=place ^ (2 * d),
        )

    def final_copy(head, d):
        peer = me ^ d
        return remote(
            final_out.at[head, peer],
            final_in.at[head, d - 1],
            final_send.at[head, d - 1],
            final_recv.at[head, d - 1],
            ctx=peer,
        )

    def last_copy(part, f, d):
        out, arrived = ((last_out_v, last_in_v), (last_out_qk, last_in_qk))[part]
        return remote(
            out.at[(far ^ f) * ctx_size + (me ^ d)],
            arrived.at[f * ctx_size + d],
            last_send.at[part],
            last_recv.at[part],
            dp=place ^ (2 * f),
            ctx=me ^ d,
        )

    def wait_last(part):
        arrived = (last_in_v, last_in_qk)[part]
        all_others = arrived.at[pl.ds(1, fars * ctx_size - 1)]
        for sem in (last_recv, last_send):
            pltpu.make_async_copy(all_others, all_others, sem.at[part]).wait()

    last_steps = [
        (f, d) for f in reversed(range(fars)) for d in reversed(range(ctx_size)) if f or d
    ]

    def group_o(chunk):
        return tuple(ref.at[chunk] for ref in (own_o, sum_out_o, sum_in_o, sum_send_o, sum_recv_o))

    def place_bit(stage):
        return lax.rem(place // 2**stage, 2)

    def stage_copy(group, stage):
        half = dp_size // 2 ** (stage + 1)
        span = pl.ds(dp_size - 2 * half, half)
        return remote(
            group[1].at[span],
            group[2].at[span],
            group[3].at[stage],
            group[4].at[stage],
            dp=place ^ 2**stage,
        )

    def stage_blocks(stage, bit):
        half = dp_size // 2 ** (stage + 1)
        first = lax.rem(place, 2**stage) + bit * 2**stage
        return [(first + 2 ** (stage + 1) * j, dp_size - 2 * half + j) for j in range(half)]

    def send_stage(group, stage):
        for block, slot in stage_blocks(stage, 1 - place_bit(stage)):
            group[1][slot] = group[0][block].astype(LOW)
        stage_copy(group, stage).start()

    def add_stage(group, stage):
        stage_copy(group, stage).wait_recv()
        for block, slot in stage_blocks(stage, place_bit(stage)):
            group[0][block] += group[2][slot].astype(WIDE)

    def final_copy_o(chunk, d):
        peer = me ^ d
        return remote(
            final_out_o.at[chunk, peer],
            final_in_o.at[chunk, d - 1],
            final_send_o.at[chunk, d - 1],
            final_recv_o.at[chunk, d - 1],
            ctx=peer,
        )

    def advance_o(chunk, stage):
        group = group_o(chunk)
        add_stage(group, stage)
        if stage + 1 < bits:
            send_stage(group, stage + 1)
            return
        total = own_o[chunk, place]
        for to in range(ctx_size):
            part = total[to * slab : (to + 1) * slab]
            final_own_o[chunk, to] = part
            final_out_o[chunk, to] = part.astype(LOW)
        for d in ctx_steps:
            final_copy_o(chunk, d).start()

    loads = (
        pltpu.make_async_copy(projector, proj, load_sem.at[0]),
        pltpu.make_async_copy(layer_input, rows_in.at[:rows], load_sem.at[1]),
        pltpu.make_async_copy(layer_grad, rows_in.at[rows:], load_sem.at[2]),
        pltpu.make_async_copy(o_hbm, out_own, load_sem.at[3]),
        pltpu.make_async_copy(g_hbm, grad_own, load_sem.at[4]),
    )
    barrier = pltpu.get_barrier_semaphore()
    greet_ctx = (1, 2) if near else tuple(ctx_steps)
    greet_dp = (0,) if near else tuple(range(bits))
    for d in greet_ctx:
        pl.semaphore_signal(barrier, inc=1, device_id={"ctx": me ^ d}, device_id_type=MESH)
    for stage in greet_dp:
        peer = place ^ 2**stage
        pl.semaphore_signal(barrier, inc=1, device_id={"dp": peer}, device_id_type=MESH)
    if near:

        @pl.when(far > 0)
        def _():
            pl.semaphore_signal(barrier, inc=1, device_id={"dp": place - 2}, device_id_type=MESH)

        @pl.when(far < fars - 1)
        def _():
            pl.semaphore_signal(barrier, inc=1, device_id={"dp": place + 2}, device_id_type=MESH)

    for load in loads:
        load.start()
    greeted = len(greet_ctx) + len(greet_dp)
    if near:
        inner = jnp.logical_and(far > 0, far < fars - 1)
        pl.semaphore_wait(barrier, greeted + 1 + inner.astype(jnp.int32))
        for index in range(2):
            for d in (1, 2):
                head_copy(0, index, d).start()
        pl.semaphore_signal(known.at[0], inc=1, device_id={"ctx": me ^ 1}, device_id_type=MESH)

        @pl.when(inner)
        def _():
            for step in (-2, 2):
                pl.semaphore_signal(
                    known.at[1], inc=1, device_id={"dp": place + step}, device_id_type=MESH
                )

        pl.semaphore_wait(known.at[0], 1)
        for index in range(2):
            head_copy(0, index, 3).start()
            local_copy(0, index).start()
    else:
        pl.semaphore_wait(barrier, greeted)
        start_head(0, range(2))
    for load in loads[:3]:
        load.wait()
    proj_acc[...] = jnp.zeros_like(proj_acc)

    @pl.loop(0, depth // DEPTH)
    def _(step):
        at = pl.ds(pl.multiple_of(step * DEPTH, DEPTH), DEPTH)
        proj_acc[...] += dot(rows_in[:, at], proj[at], ((1,), (0,)))

    reduced[mine] = proj_acc[:rows].astype(LOW)
    for d in red_steps:
        reduced_copy(d).start()
    start_head(0, range(2, count))
    reduced_grad[...] = proj_acc[rows:].astype(LOW)
    for load in loads[3:]:
        load.wait()
    rgrad_t = reduced_grad[...].T
    part_width = own_o.shape[3]
    for chunk in range(CHUNKS):
        at = slice(chunk * part_width, (chunk + 1) * part_width)
        for part in range(dp_size):
            span = slice(part * piece, (part + 1) * piece)
            own_o[chunk, part] = dot(rgrad_t[span], out_own[:, at], ((1,), (0,)))
        send_stage(group_o(chunk), 0)

    lane = lax.broadcasted_iota(jnp.int32, (rows, BLOCK), 1)
    table = jnp.zeros((rows, BLOCK), WIDE)
    for head in range(heads * ctx_size):
        span = slice(head * width, (head + 1) * width)
        product = grad_own[:, span].astype(WIDE) * out_own[:, span].astype(WIDE)
        table = jnp.where(lane == head, jnp.sum(product, axis=1, keepdims=True), table)
    table = table.T
    delta_out[...] = jnp.zeros_like(delta_out)
    for owner in range(ctx_size):
        delta_out[owner, :heads] = table[owner * heads : (owner + 1) * heads]
    delta_in[me] = delta_out[me]
    for d in ctx_steps:
        delta_copy(d).start()
    if near:
        pl.semaphore_wait(known.at[1], 1)
    for chunk in range(2):
        advance_o(chunk, 0)

    def complete_o(chunks):
        for chunk in chunks:
            for stage in range(2, bits):
                advance_o(chunk, stage)

    for d in red_steps:
        reduced_copy(d).wait_recv()
        if passing:
            pass_copy(d).start()
    for head in range(1, heads):
        start_head(head, range(count))
    advance_o(0, 1)
    advance_o(2, 0)

    def gather_reduced():
        advance_o(1, 1)
        advance_o(3, 0)
        for d in ctx_steps:
            delta_copy(d).wait_recv()
        delta_rows[...] = jnp.concatenate([delta_in[owner] for owner in range(ctx_size)], axis=1)
        if passing:
            for d in red_steps:
                pass_copy(d).wait_recv()
        turned = reduced[...].T
        for part in range(dp_size):
            block = turned[part * piece : (part + 1) * piece]
            reduced_t[part % 2, (part // 2) * piece : (part // 2 + 1) * piece] = block

    def keep(head, total, lanes):
        for f in range(fars):
            block = total[f * piece : (f + 1) * piece]
            total_ref[head, f, :, lanes] = block
            far_out[head, f, :, lanes] = block.astype(LOW)

    def send_last(total, part):
        own, out = ((last_own_v, last_out_v), (last_own_qk, last_out_qk))[part]
        for f in range(fars):
            for to in range(ctx_size):
                first = f * piece + to * slab
                block = total[first : first + slab]
                own[f, to] = block
                out[f * ctx_size + to] = block.astype(LOW)
        for f, d in last_steps:
            last_copy(part, f, d).start()

    def finish(head):
        total = total_ref[head, far]
        for d in range(1, fars):
            for part in range(2):
                far_copy(head, part, d).wait_recv()
            total += far_in[head, d - 1].astype(WIDE)
        for to in range(ctx_size):
            block = total[to * slab : (to + 1) * slab]
            final_own[head, to] = block
            final_out[head, to] = block.astype(LOW)
        for d in ctx_steps:
            final_copy(head, d).start()

    @pl.loop(0, heads)
    def _(head):
        wait_head(head, range(3))
        sums = sums_ref[pl.ds(me * heads + head, 1), :]
        value_products(arrays, head, sums, prob_ref, dv_low)

        @pl.when(head == 0)
        def _():
            gather_reduced()

        @pl.when(head == 1)
        def _():
            advance_o(3, 1)

        low = dv_low[...]
        core_out_v[head] = dot(reduced_t[1 - core], low, ((1,), (0,))).astype(LOW)
        core_copy(head, 0).start()
        mine_v[...] = dot(reduced_t[core], low, ((1,), (0,)))

        def add_values():
            core_copy(head, 0).wait_recv()
            total = mine_v[...] + core_in_v[head].astype(WIDE)

            @pl.when(head < last)
            def _():
                keep(head, total, slice(both, both + width))
                for d in reversed(range(1, fars)):
                    far_copy(head, 0, d).start()

            @pl.when(head == last)
            def _():
                send_last(total, 0)

        wait_head(head, range(3, count))
        deltas = delta_rows[pl.ds(head, 1), :]
        score_products(arrays, head, deltas, prob_ref, acc, qk_low, add_values)
        low = qk_low[...]
        core_out_qk[head] = dot(reduced_t[1 - core], low, ((1,), (0,))).astype(LOW)
        core_copy(head, 1).start()
        joined = dot(reduced_t[core], low, ((1,), (0,)))
        core_copy(head, 1).wait_recv()
        total = joined + core_in_qk[head].astype(WIDE)

        @pl.when(head < last)
        def _():
            keep(head, total, slice(0, both))
            for d in reversed(range(1, fars)):
                far_copy(head, 1, d).start()

        @pl.when(head == last)
        def _():
            send_last(total, 1)

        @pl.when(head == 0)
        def _():
            advance_o(2, 1)

        @pl.when(head == max(last - 1, 1))
        def _():
            complete_o(range(CHUNKS))

        @pl.when(head < last)
        def _():
            for part in range(2):
                core_copy(head, part).wait_send()
            wait_sent(head)

    for d in red_steps:
        reduced_copy(d).wait_send()
    if passing:
        for d in red_steps:
            pass_copy(d).wait_send()
    for d in ctx_steps:
        delta_copy(d).wait_send()
    for chunk in range(CHUNKS):
        for stage in range(bits):
            stage_copy(group_o(chunk), stage).wait_send()
    for head in range(last):
        finish(head)
    for part in range(2):
        core_copy(last, part).wait_send()
    wait_sent(last)

    for chunk in range(CHUNKS):
        at = slice(chunk * part_width, (chunk + 1) * part_width)
        total = final_own_o[chunk, me]
        for d in ctx_steps:
            final_copy_o(chunk, d).wait()
            total += final_in_o[chunk, d - 1].astype(WIDE)
        out_ref[3, :, at] = total

    for head in range(last):
        for d in range(1, fars):
            for part in range(2):
                far_copy(head, part, d).wait_send()
        for d in range(ctx_size):
            if d:
                final_copy(head, d).wait()
                block = final_in[head, d - 1].astype(WIDE)
            else:
                block = final_own[head, me]
            for index in range(3):
                span = slice(index * width, (index + 1) * width)
                out_ref[index, :, columns(me ^ d, head)] = block[:, span]

    for part, own, arrived, first in ((0, last_own_v, last_in_v, 2), (1, last_own_qk, last_in_qk, 0)):
        wait_last(part)
        for d in range(ctx_size):
            total = None if d else own[far, me]
            for f in range(fars):
                if f or d:
                    block = arrived[f * ctx_size + d].astype(WIDE)
                    total = block if total is None else total + block
            for index in range(own.shape[3] // width):
                span = slice(index * width, (index + 1) * width)
                out_ref[first + index, :, columns(me ^ d, last)] = total[:, span]


def on_device(
    dp_size,
    ctx_size,
    layer_input,
    queries,
    key_rows,
    value_rows,
    attn_out,
    out_grad,
    layer_grad,
    logsum,
    projector,
):
    rows, features = queries.shape[1:]
    all_heads, tokens = logsum.shape[1:]
    heads = all_heads // ctx_size
    width = features // all_heads
    depth, rank = projector.shape
    bits = dp_size.bit_length() - 1
    fars = dp_size // 2
    piece = rank // dp_size
    slab = piece // ctx_size
    padded = -(-heads // 8) * 8
    half = rank // 2
    both = 2 * width
    three = 3 * width
    part_width = features // CHUNKS
    others = ctx_size - 1
    dma = pltpu.SemaphoreType.DMA
    anywhere = pl.BlockSpec(memory_space=pl.ANY)
    in_vmem = pl.BlockSpec(memory_space=pltpu.VMEM)
    return pl.pallas_call(
        functools.partial(kernel, dp_size, ctx_size),
        out_shape=pltpu.VMEM((4, slab, features), WIDE),
        in_specs=[anywhere] * 7 + [in_vmem, anywhere],
        out_specs=in_vmem,
        scratch_shapes=[
            pltpu.VMEM((4, heads, tokens, width), LOW),
            pltpu.VMEM((2 * rows, depth), LOW),
            pltpu.VMEM((depth, rank), LOW),
            pltpu.VMEM((2 * rows, rank), WIDE),
            pltpu.VMEM((rows, features), LOW),
            pltpu.VMEM((rows, features), LOW),
            pltpu.VMEM((tokens, rank), LOW),
            pltpu.VMEM((2, half, tokens), LOW),
            pltpu.VMEM((rows, rank), LOW),
            pltpu.VMEM((ctx_size, padded, rows), WIDE),
            pltpu.VMEM((ctx_size, padded, rows), WIDE),
            pltpu.VMEM((padded, tokens), WIDE),
            pltpu.VMEM((tokens, tokens), WIDE),
            pltpu.VMEM((tokens, width), WIDE),
            pltpu.VMEM((tokens, width), LOW),
            pltpu.VMEM((tokens, both), LOW),
            pltpu.VMEM((half, width), WIDE),
            pltpu.VMEM((heads, half, width), LOW),
            pltpu.VMEM((heads, half, width), LOW),
            pltpu.VMEM((heads, half, both), LOW),
            pltpu.VMEM((heads, half, both), LOW),
            pltpu.VMEM((heads, fars, piece, three), WIDE),
            pltpu.VMEM((heads, fars, piece, three), LOW),
            pltpu.VMEM((heads, fars - 1, piece, three), LOW),
            pltpu.VMEM((heads, ctx_size, slab, three), WIDE),
            pltpu.VMEM((heads, ctx_size, slab, three), LOW),
            pltpu.VMEM((heads, others, slab, three), LOW),
            pltpu.VMEM((fars, ctx_size, slab, width), WIDE),
            pltpu.VMEM((fars * ctx_size, slab, width), LOW),
            pltpu.VMEM((fars * ctx_size, slab, width), LOW),
            pltpu.VMEM((fars, ctx_size, slab, both), WIDE),
            pltpu.VMEM((fars * ctx_size, slab, both), LOW),
            pltpu.VMEM((fars * ctx_size, slab, both), LOW),
            pltpu.VMEM((CHUNKS, dp_size, piece, part_width), WIDE),
            pltpu.VMEM((CHUNKS, dp_size - 1, piece, part_width), LOW),
            pltpu.VMEM((CHUNKS, dp_size - 1, piece, part_width), LOW),
            pltpu.VMEM((CHUNKS, ctx_size, slab, part_width), WIDE),
            pltpu.VMEM((CHUNKS, ctx_size, slab, part_width), LOW),
            pltpu.VMEM((CHUNKS, others, slab, part_width), LOW),
            dma((5,)),
            dma((heads, 4)),
            dma((heads, 4, others)),
            dma((heads, 4, others)),
            dma((others,)),
            dma((others,)),
            dma((2,)),
            dma((2,)),
            dma((others,)),
            dma((others,)),
            dma((heads, 2)),
            dma((heads, 2)),
            dma((heads, 2, fars - 1)),
            dma((heads, 2, fars - 1)),
            dma((heads, others)),
            dma((heads, others)),
            dma((2,)),
            dma((2,)),
            dma((CHUNKS, bits)),
            dma((CHUNKS, bits)),
            dma((CHUNKS, others)),
            dma((CHUNKS, others)),
            pltpu.SemaphoreType.REGULAR((2,)),
        ],
        compiler_params=pltpu.CompilerParams(
            collective_id=0, has_side_effects=True, vmem_limit_bytes=56 * 1024 * 1024
        ),
    )(
        layer_input[0],
        queries[0],
        key_rows[0],
        value_rows[0],
        attn_out[0],
        out_grad[0],
        layer_grad[0],
        logsum[0],
        projector,
    )


def solution(mesh):
    rows = P("dp", "ctx", None)
    placed = (rows,) * 7 + (P("dp", None, None), P())
    return jax.shard_map(
        functools.partial(on_device, mesh.shape["dp"], mesh.shape["ctx"]),
        mesh=mesh,
        in_specs=placed,
        out_specs=P(None, ("dp", "ctx"), None),
        check_vma=False,
    )
```

```python
import functools
import math

import jax
import jax.numpy as jnp
from jax import lax
from jax.experimental import pallas as pl
from jax.experimental.pallas import tpu as pltpu
from jax.sharding import PartitionSpec as P

BLOCK = 128
DEPTH = 512
CHUNKS = 4
MESH = pl.DeviceIdType.MESH
LOW, WIDE = jnp.bfloat16, jnp.float32


def dot(left, right, dims):
    return lax.dot_general(left, right, (dims, ((), ())), preferred_element_type=jnp.float32)


def value_products(arrays, head, sums, prob_ref, dv_low):
    q_ref, k_ref, g_ref = (arrays.at[index, head] for index in range(3))
    tokens, width = q_ref.shape
    scaling = 1.0 / math.sqrt(width)
    row = lax.broadcasted_iota(jnp.int32, (BLOCK, BLOCK), 0)
    col = lax.broadcasted_iota(jnp.int32, (BLOCK, BLOCK), 1)
    causal = row <= col
    for start in range(0, tokens, BLOCK):
        span = slice(start, start + BLOCK)
        scores = dot(k_ref[span], q_ref[start:], ((1,), (1,))) * scaling
        prob = jnp.exp(scores - sums[:, start:])
        diagonal = jnp.where(causal, prob[:, :BLOCK], 0.0)
        if start + BLOCK < tokens:
            prob = jnp.concatenate([diagonal, prob[:, BLOCK:]], axis=1)
        else:
            prob = diagonal
        prob_ref[span, start:] = prob
        dv_low[span] = dot(prob.astype(LOW), g_ref[start:], ((1,), (0,))).astype(LOW)


def score_products(arrays, head, deltas, prob_ref, acc, qk_low, between):
    q_ref, k_ref, g_ref, v_ref = (arrays.at[index, head] for index in range(4))
    tokens, width = q_ref.shape
    scaling = 1.0 / math.sqrt(width)
    for start in range(0, tokens, BLOCK):
        span = slice(start, start + BLOCK)
        dprob = dot(v_ref[span], g_ref[start:], ((1,), (1,)))
        dscore = prob_ref[span, start:] * (dprob - deltas[:, start:]) * scaling
        score_low = dscore.astype(LOW)
        dquery = dot(score_low, k_ref[span], ((0,), (0,)))
        if start == 0:
            acc[...] = dquery
        else:
            acc[start:] += dquery
        qk_low[span, :width] = acc[span].astype(LOW)
        qk_low[span, width:] = dot(score_low, q_ref[start:], ((1,), (0,))).astype(LOW)
        if start == BLOCK:
            between()


def kernel(
    dp_size,
    ctx_size,
    layer_input,
    q_hbm,
    k_hbm,
    v_hbm,
    o_hbm,
    g_hbm,
    layer_grad,
    sums_ref,
    projector,
    out_ref,
    arrays,
    rows_in,
    proj,
    proj_acc,
    grad_own,
    out_own,
    reduced,
    reduced_t,
    reduced_grad,
    delta_out,
    delta_in,
    delta_rows,
    prob_ref,
    acc,
    dv_low,
    qk_low,
    mine_v,
    core_out_v,
    core_in_v,
    core_out_qk,
    core_in_qk,
    total_ref,
    far_out,
    far_in,
    final_own,
    final_out,
    final_in,
    last_own_v,
    last_out_v,
    last_in_v,
    last_own_qk,
    last_out_qk,
    last_in_qk,
    own_o,
    sum_out_o,
    sum_in_o,
    final_own_o,
    final_out_o,
    final_in_o,
    load_sem,
    local_sem,
    head_send,
    head_recv,
    red_send,
    red_recv,
    pass_send,
    pass_recv,
    delta_send,
    delta_recv,
    core_send,
    core_recv,
    far_send,
    far_recv,
    final_send,
    final_recv,
    last_send,
    last_recv,
    sum_send_o,
    sum_recv_o,
    final_send_o,
    final_recv_o,
    known,
):
    me = lax.axis_index("ctx")
    place = lax.axis_index("dp")
    bits = dp_size.bit_length() - 1
    fars = dp_size // 2
    core = lax.rem(place, 2)
    far = place // 2
    sources = (q_hbm, k_hbm, g_hbm, v_hbm)
    count = len(sources)
    heads = arrays.shape[1]
    last = heads - 1
    rows = q_hbm.shape[0]
    width = arrays.shape[3]
    depth = projector.shape[0]
    rank = projector.shape[1]
    piece = rank // dp_size
    slab = piece // ctx_size
    both = 2 * width
    passing = ctx_size == 4
    near = ctx_size == 4 and fars == 4
    mine = pl.ds(pl.multiple_of(me * rows, 16), rows)
    ctx_steps = range(1, ctx_size)

    def columns(owner, head):
        return pl.ds(pl.multiple_of((owner * heads + head) * width, width), width)

    def remote(src, dst, send, recv, **where):
        return pltpu.make_async_remote_copy(
            src_ref=src,
            dst_ref=dst,
            send_sem=send,
            recv_sem=recv,
            device_id=where,
            device_id_type=MESH,
        )

    def local_copy(head, index):
        return pltpu.make_async_copy(
            sources[index].at[:, columns(me, head)],
            arrays.at[index, head, mine],
            local_sem.at[head, index],
        )

    def head_copy(head, index, d):
        peer = me ^ d
        return remote(
            sources[index].at[:, columns(peer, head)],
            arrays.at[index, head, mine],
            head_send.at[head, index, d - 1],
            head_recv.at[head, index, d - 1],
            ctx=peer,
        )

    def start_head(head, indices):
        for index in indices:
            for d in reversed(ctx_steps):
                head_copy(head, index, d).start()
        for index in indices:
            local_copy(head, index).start()

    def wait_sent(head):
        for index in range(count):
            for d in ctx_steps:
                head_copy(head, index, d).wait_send()

    def wait_head(head, indices):
        for index in indices:
            local_copy(head, index).wait()
            for d in ctx_steps:
                head_copy(head, index, d).wait_recv()

    red_steps = (1, 2) if passing else tuple(ctx_steps)

    def reduced_copy(d):
        return remote(
            reduced.at[mine],
            reduced.at[mine],
            red_send.at[d - 1],
            red_recv.at[d - 1],
            ctx=me ^ d,
        )

    def pass_copy(d):
        half = rows // 2
        at = pl.ds(pl.multiple_of((me ^ d) * rows + (d - 1) * half, 16), half)
        return remote(
            reduced.at[at],
            reduced.at[at],
            pass_send.at[d - 1],
            pass_recv.at[d - 1],
            ctx=me ^ (3 - d),
        )

    def delta_copy(d):
        peer = me ^ d
        return remote(
            delta_out.at[peer],
            delta_in.at[me],
            delta_send.at[d - 1],
            delta_recv.at[d - 1],
            ctx=peer,
        )

    def core_copy(head, part):
        out, arrived = ((core_out_v, core_in_v), (core_out_qk, core_in_qk))[part]
        return remote(
            out.at[head],
            arrived.at[head],
            core_send.at[head, part],
            core_recv.at[head, part],
            dp=place ^ 1,
        )

    def far_copy(head, part, d):
        lanes = (pl.ds(both, width), pl.ds(0, both))[part]
        return remote(
            far_out.at[head, far ^ d, :, lanes],
            far_in.at[head, d - 1, :, lanes],
            far_send.at[head, part, d - 1],
            far_recv.at[head, part, d - 1],
            dp=place ^ (2 * d),
        )

    def final_copy(head, d):
        peer = me ^ d
        return remote(
            final_out.at[head, peer],
            final_in.at[head, d - 1],
            final_send.at[head, d - 1],
            final_recv.at[head, d - 1],
            ctx=peer,
        )

    def last_copy(part, f, d):
        out, arrived = ((last_out_v, last_in_v), (last_out_qk, last_in_qk))[part]
        return remote(
            out.at[(far ^ f) * ctx_size + (me ^ d)],
            arrived.at[f * ctx_size + d],
            last_send.at[part],
            last_recv.at[part],
            dp=place ^ (2 * f),
            ctx=me ^ d,
        )

    def wait_last(part):
        arrived = (last_in_v, last_in_qk)[part]
        all_others = arrived.at[pl.ds(1, fars * ctx_size - 1)]
        for sem in (last_recv, last_send):
            pltpu.make_async_copy(all_others, all_others, sem.at[part]).wait()

    last_steps = [
        (f, d) for f in reversed(range(fars)) for d in reversed(range(ctx_size)) if f or d
    ]

    def group_o(chunk):
        return tuple(ref.at[chunk] for ref in (own_o, sum_out_o, sum_in_o, sum_send_o, sum_recv_o))

    def place_bit(stage):
        return lax.rem(place // 2**stage, 2)

    def stage_copy(group, stage):
        half = dp_size // 2 ** (stage + 1)
        span = pl.ds(dp_size - 2 * half, half)
        return remote(
            group[1].at[span],
            group[2].at[span],
            group[3].at[stage],
            group[4].at[stage],
            dp=place ^ 2**stage,
        )

    def stage_blocks(stage, bit):
        half = dp_size // 2 ** (stage + 1)
        first = lax.rem(place, 2**stage) + bit * 2**stage
        return [(first + 2 ** (stage + 1) * j, dp_size - 2 * half + j) for j in range(half)]

    def send_stage(group, stage):
        for block, slot in stage_blocks(stage, 1 - place_bit(stage)):
            group[1][slot] = group[0][block].astype(LOW)
        stage_copy(group, stage).start()

    def add_stage(group, stage):
        stage_copy(group, stage).wait_recv()
        for block, slot in stage_blocks(stage, place_bit(stage)):
            group[0][block] += group[2][slot].astype(WIDE)

    def final_copy_o(chunk, d):
        peer = me ^ d
        return remote(
            final_out_o.at[chunk, peer],
            final_in_o.at[chunk, d - 1],
            final_send_o.at[chunk, d - 1],
            final_recv_o.at[chunk, d - 1],
            ctx=peer,
        )

    def advance_o(chunk, stage):
        group = group_o(chunk)
        add_stage(group, stage)
        if stage + 1 < bits:
            send_stage(group, stage + 1)
            return
        total = own_o[chunk, place]
        for to in range(ctx_size):
            part = total[to * slab : (to + 1) * slab]
            final_own_o[chunk, to] = part
            final_out_o[chunk, to] = part.astype(LOW)
        for d in ctx_steps:
            final_copy_o(chunk, d).start()

    loads = (
        pltpu.make_async_copy(projector, proj, load_sem.at[0]),
        pltpu.make_async_copy(layer_input, rows_in.at[:rows], load_sem.at[1]),
        pltpu.make_async_copy(layer_grad, rows_in.at[rows:], load_sem.at[2]),
        pltpu.make_async_copy(o_hbm, out_own, load_sem.at[3]),
        pltpu.make_async_copy(g_hbm, grad_own, load_sem.at[4]),
    )
    barrier = pltpu.get_barrier_semaphore()
    greet_ctx = (1, 2) if near else tuple(ctx_steps)
    greet_dp = (0,) if near else tuple(range(bits))
    for d in greet_ctx:
        pl.semaphore_signal(barrier, inc=1, device_id={"ctx": me ^ d}, device_id_type=MESH)
    for stage in greet_dp:
        peer = place ^ 2**stage
        pl.semaphore_signal(barrier, inc=1, device_id={"dp": peer}, device_id_type=MESH)
    if near:

        @pl.when(far > 0)
        def _():
            pl.semaphore_signal(barrier, inc=1, device_id={"dp": place - 2}, device_id_type=MESH)

        @pl.when(far < fars - 1)
        def _():
            pl.semaphore_signal(barrier, inc=1, device_id={"dp": place + 2}, device_id_type=MESH)

    for load in loads:
        load.start()
    greeted = len(greet_ctx) + len(greet_dp)
    if near:
        inner = jnp.logical_and(far > 0, far < fars - 1)
        pl.semaphore_wait(barrier, greeted + 1 + inner.astype(jnp.int32))
        for index in range(2):
            for d in (1, 2):
                head_copy(0, index, d).start()
        pl.semaphore_signal(known.at[0], inc=1, device_id={"ctx": me ^ 1}, device_id_type=MESH)

        @pl.when(inner)
        def _():
            for step in (-2, 2):
                pl.semaphore_signal(
                    known.at[1], inc=1, device_id={"dp": place + step}, device_id_type=MESH
                )

        pl.semaphore_wait(known.at[0], 1)
        for index in range(2):
            head_copy(0, index, 3).start()
            local_copy(0, index).start()
    else:
        pl.semaphore_wait(barrier, greeted)
        start_head(0, range(2))
    for load in loads[:3]:
        load.wait()
    proj_acc[...] = jnp.zeros_like(proj_acc)

    @pl.loop(0, depth // DEPTH)
    def _(step):
        at = pl.ds(pl.multiple_of(step * DEPTH, DEPTH), DEPTH)
        proj_acc[...] += dot(rows_in[:, at], proj[at], ((1,), (0,)))

    reduced[mine] = proj_acc[:rows].astype(LOW)
    for d in red_steps:
        reduced_copy(d).start()
    start_head(0, range(2, count))
    reduced_grad[...] = proj_acc[rows:].astype(LOW)
    for load in loads[3:]:
        load.wait()
    rgrad_t = reduced_grad[...].T
    part_width = own_o.shape[3]
    for chunk in range(CHUNKS):
        at = slice(chunk * part_width, (chunk + 1) * part_width)
        for part in range(dp_size):
            span = slice(part * piece, (part + 1) * piece)
            own_o[chunk, part] = dot(rgrad_t[span], out_own[:, at], ((1,), (0,)))
        send_stage(group_o(chunk), 0)

    if near:
        pl.semaphore_wait(known.at[1], 1)
    for chunk in range(2):
        advance_o(chunk, 0)

    def complete_o(chunks):
        for chunk in chunks:
            for stage in range(2, bits):
                advance_o(chunk, stage)

    lane = lax.broadcasted_iota(jnp.int32, (rows, BLOCK), 1)
    table = jnp.zeros((rows, BLOCK), WIDE)
    for head in range(heads * ctx_size):
        span = slice(head * width, (head + 1) * width)
        product = grad_own[:, span].astype(WIDE) * out_own[:, span].astype(WIDE)
        table = jnp.where(lane == head, jnp.sum(product, axis=1, keepdims=True), table)
    table = table.T
    delta_out[...] = jnp.zeros_like(delta_out)
    for owner in range(ctx_size):
        delta_out[owner, :heads] = table[owner * heads : (owner + 1) * heads]
    delta_in[me] = delta_out[me]
    for d in ctx_steps:
        delta_copy(d).start()
    for d in red_steps:
        reduced_copy(d).wait_recv()
        if passing:
            pass_copy(d).start()
    for head in range(1, heads):
        start_head(head, range(count))
    advance_o(0, 1)
    advance_o(2, 0)

    def gather_reduced():
        advance_o(1, 1)
        advance_o(3, 0)
        for d in ctx_steps:
            delta_copy(d).wait_recv()
        delta_rows[...] = jnp.concatenate([delta_in[owner] for owner in range(ctx_size)], axis=1)
        if passing:
            for d in red_steps:
                pass_copy(d).wait_recv()
        turned = reduced[...].T
        for part in range(dp_size):
            block = turned[part * piece : (part + 1) * piece]
            reduced_t[part % 2, (part // 2) * piece : (part // 2 + 1) * piece] = block

    def keep(head, total, lanes):
        for f in range(fars):
            block = total[f * piece : (f + 1) * piece]
            total_ref[head, f, :, lanes] = block
            far_out[head, f, :, lanes] = block.astype(LOW)

    def send_last(total, part):
        own, out = ((last_own_v, last_out_v), (last_own_qk, last_out_qk))[part]
        for f in range(fars):
            for to in range(ctx_size):
                first = f * piece + to * slab
                block = total[first : first + slab]
                own[f, to] = block
                out[f * ctx_size + to] = block.astype(LOW)
        for f, d in last_steps:
            last_copy(part, f, d).start()

    def finish(head):
        total = total_ref[head, far]
        for d in range(1, fars):
            for part in range(2):
                far_copy(head, part, d).wait_recv()
            total += far_in[head, d - 1].astype(WIDE)
        for to in range(ctx_size):
            block = total[to * slab : (to + 1) * slab]
            final_own[head, to] = block
            final_out[head, to] = block.astype(LOW)
        for d in ctx_steps:
            final_copy(head, d).start()

    @pl.loop(0, heads)
    def _(head):
        wait_head(head, range(3))
        sums = sums_ref[pl.ds(me * heads + head, 1), :]
        value_products(arrays, head, sums, prob_ref, dv_low)

        @pl.when(head == 0)
        def _():
            gather_reduced()

        @pl.when(head == 1)
        def _():
            advance_o(3, 1)

        low = dv_low[...]
        core_out_v[head] = dot(reduced_t[1 - core], low, ((1,), (0,))).astype(LOW)
        core_copy(head, 0).start()
        mine_v[...] = dot(reduced_t[core], low, ((1,), (0,)))

        def add_values():
            core_copy(head, 0).wait_recv()
            total = mine_v[...] + core_in_v[head].astype(WIDE)

            @pl.when(head < last)
            def _():
                keep(head, total, slice(both, both + width))
                for d in reversed(range(1, fars)):
                    far_copy(head, 0, d).start()

            @pl.when(head == last)
            def _():
                send_last(total, 0)

        wait_head(head, range(3, count))
        deltas = delta_rows[pl.ds(head, 1), :]
        score_products(arrays, head, deltas, prob_ref, acc, qk_low, add_values)
        low = qk_low[...]
        core_out_qk[head] = dot(reduced_t[1 - core], low, ((1,), (0,))).astype(LOW)
        core_copy(head, 1).start()
        joined = dot(reduced_t[core], low, ((1,), (0,)))
        core_copy(head, 1).wait_recv()
        total = joined + core_in_qk[head].astype(WIDE)

        @pl.when(head < last)
        def _():
            keep(head, total, slice(0, both))
            for d in reversed(range(1, fars)):
                far_copy(head, 1, d).start()

        @pl.when(head == last)
        def _():
            send_last(total, 1)

        @pl.when(head == 0)
        def _():
            advance_o(2, 1)

        @pl.when(head == max(last - 1, 1))
        def _():
            complete_o(range(CHUNKS))

        @pl.when(head < last)
        def _():
            for part in range(2):
                core_copy(head, part).wait_send()
            wait_sent(head)

    for d in red_steps:
        reduced_copy(d).wait_send()
    if passing:
        for d in red_steps:
            pass_copy(d).wait_send()
    for d in ctx_steps:
        delta_copy(d).wait_send()
    for chunk in range(CHUNKS):
        for stage in range(bits):
            stage_copy(group_o(chunk), stage).wait_send()
    for head in range(last):
        finish(head)
    for part in range(2):
        core_copy(last, part).wait_send()
    wait_sent(last)

    for chunk in range(CHUNKS):
        at = slice(chunk * part_width, (chunk + 1) * part_width)
        total = final_own_o[chunk, me]
        for d in ctx_steps:
            final_copy_o(chunk, d).wait()
            total += final_in_o[chunk, d - 1].astype(WIDE)
        out_ref[3, :, at] = total

    for head in range(last):
        for d in range(1, fars):
            for part in range(2):
                far_copy(head, part, d).wait_send()
        for d in range(ctx_size):
            if d:
                final_copy(head, d).wait()
                block = final_in[head, d - 1].astype(WIDE)
            else:
                block = final_own[head, me]
            for index in range(3):
                span = slice(index * width, (index + 1) * width)
                out_ref[index, :, columns(me ^ d, head)] = block[:, span]

    for part, own, arrived, first in ((0, last_own_v, last_in_v, 2), (1, last_own_qk, last_in_qk, 0)):
        wait_last(part)
        for d in range(ctx_size):
            total = None if d else own[far, me]
            for f in range(fars):
                if f or d:
                    block = arrived[f * ctx_size + d].astype(WIDE)
                    total = block if total is None else total + block
            for index in range(own.shape[3] // width):
                span = slice(index * width, (index + 1) * width)
                out_ref[first + index, :, columns(me ^ d, last)] = total[:, span]


def on_device(
    dp_size,
    ctx_size,
    layer_input,
    queries,
    key_rows,
    value_rows,
    attn_out,
    out_grad,
    layer_grad,
    logsum,
    projector,
):
    rows, features = queries.shape[1:]
    all_heads, tokens = logsum.shape[1:]
    heads = all_heads // ctx_size
    width = features // all_heads
    depth, rank = projector.shape
    bits = dp_size.bit_length() - 1
    fars = dp_size // 2
    piece = rank // dp_size
    slab = piece // ctx_size
    padded = -(-heads // 8) * 8
    half = rank // 2
    both = 2 * width
    three = 3 * width
    part_width = features // CHUNKS
    others = ctx_size - 1
    dma = pltpu.SemaphoreType.DMA
    anywhere = pl.BlockSpec(memory_space=pl.ANY)
    in_vmem = pl.BlockSpec(memory_space=pltpu.VMEM)
    return pl.pallas_call(
        functools.partial(kernel, dp_size, ctx_size),
        out_shape=pltpu.VMEM((4, slab, features), WIDE),
        in_specs=[anywhere] * 7 + [in_vmem, anywhere],
        out_specs=in_vmem,
        scratch_shapes=[
            pltpu.VMEM((4, heads, tokens, width), LOW),
            pltpu.VMEM((2 * rows, depth), LOW),
            pltpu.VMEM((depth, rank), LOW),
            pltpu.VMEM((2 * rows, rank), WIDE),
            pltpu.VMEM((rows, features), LOW),
            pltpu.VMEM((rows, features), LOW),
            pltpu.VMEM((tokens, rank), LOW),
            pltpu.VMEM((2, half, tokens), LOW),
            pltpu.VMEM((rows, rank), LOW),
            pltpu.VMEM((ctx_size, padded, rows), WIDE),
            pltpu.VMEM((ctx_size, padded, rows), WIDE),
            pltpu.VMEM((padded, tokens), WIDE),
            pltpu.VMEM((tokens, tokens), WIDE),
            pltpu.VMEM((tokens, width), WIDE),
            pltpu.VMEM((tokens, width), LOW),
            pltpu.VMEM((tokens, both), LOW),
            pltpu.VMEM((half, width), WIDE),
            pltpu.VMEM((heads, half, width), LOW),
            pltpu.VMEM((heads, half, width), LOW),
            pltpu.VMEM((heads, half, both), LOW),
            pltpu.VMEM((heads, half, both), LOW),
            pltpu.VMEM((heads, fars, piece, three), WIDE),
            pltpu.VMEM((heads, fars, piece, three), LOW),
            pltpu.VMEM((heads, fars - 1, piece, three), LOW),
            pltpu.VMEM((heads, ctx_size, slab, three), WIDE),
            pltpu.VMEM((heads, ctx_size, slab, three), LOW),
            pltpu.VMEM((heads, others, slab, three), LOW),
            pltpu.VMEM((fars, ctx_size, slab, width), WIDE),
            pltpu.VMEM((fars * ctx_size, slab, width), LOW),
            pltpu.VMEM((fars * ctx_size, slab, width), LOW),
            pltpu.VMEM((fars, ctx_size, slab, both), WIDE),
            pltpu.VMEM((fars * ctx_size, slab, both), LOW),
            pltpu.VMEM((fars * ctx_size, slab, both), LOW),
            pltpu.VMEM((CHUNKS, dp_size, piece, part_width), WIDE),
            pltpu.VMEM((CHUNKS, dp_size - 1, piece, part_width), LOW),
            pltpu.VMEM((CHUNKS, dp_size - 1, piece, part_width), LOW),
            pltpu.VMEM((CHUNKS, ctx_size, slab, part_width), WIDE),
            pltpu.VMEM((CHUNKS, ctx_size, slab, part_width), LOW),
            pltpu.VMEM((CHUNKS, others, slab, part_width), LOW),
            dma((5,)),
            dma((heads, 4)),
            dma((heads, 4, others)),
            dma((heads, 4, others)),
            dma((others,)),
            dma((others,)),
            dma((2,)),
            dma((2,)),
            dma((others,)),
            dma((others,)),
            dma((heads, 2)),
            dma((heads, 2)),
            dma((heads, 2, fars - 1)),
            dma((heads, 2, fars - 1)),
            dma((heads, others)),
            dma((heads, others)),
            dma((2,)),
            dma((2,)),
            dma((CHUNKS, bits)),
            dma((CHUNKS, bits)),
            dma((CHUNKS, others)),
            dma((CHUNKS, others)),
            pltpu.SemaphoreType.REGULAR((2,)),
        ],
        compiler_params=pltpu.CompilerParams(
            collective_id=0, has_side_effects=True, vmem_limit_bytes=56 * 1024 * 1024
        ),
    )(
        layer_input[0],
        queries[0],
        key_rows[0],
        value_rows[0],
        attn_out[0],
        out_grad[0],
        layer_grad[0],
        logsum[0],
        projector,
    )


def solution(mesh):
    rows = P("dp", "ctx", None)
    placed = (rows,) * 7 + (P("dp", None, None), P())
    return jax.shard_map(
        functools.partial(on_device, mesh.shape["dp"], mesh.shape["ctx"]),
        mesh=mesh,
        in_specs=placed,
        out_specs=P(None, ("dp", "ctx"), None),
        check_vma=False,
    )
```

```python
import functools
import math

import jax
import jax.numpy as jnp
from jax import lax
from jax.experimental import pallas as pl
from jax.experimental.pallas import tpu as pltpu
from jax.sharding import PartitionSpec as P

BLOCK = 128
DEPTH = 512
CHUNKS = 4
MESH = pl.DeviceIdType.MESH
LOW, WIDE = jnp.bfloat16, jnp.float32


def dot(left, right, dims):
    return lax.dot_general(left, right, (dims, ((), ())), preferred_element_type=jnp.float32)


def value_products(arrays, head, sums, prob_ref, dv_low):
    q_ref, k_ref, g_ref = (arrays.at[index, head] for index in range(3))
    tokens, width = q_ref.shape
    scaling = 1.0 / math.sqrt(width)
    row = lax.broadcasted_iota(jnp.int32, (BLOCK, BLOCK), 0)
    col = lax.broadcasted_iota(jnp.int32, (BLOCK, BLOCK), 1)
    causal = row <= col
    for start in range(0, tokens, BLOCK):
        span = slice(start, start + BLOCK)
        scores = dot(k_ref[span], q_ref[start:], ((1,), (1,))) * scaling
        prob = jnp.exp(scores - sums[:, start:])
        diagonal = jnp.where(causal, prob[:, :BLOCK], 0.0)
        if start + BLOCK < tokens:
            prob = jnp.concatenate([diagonal, prob[:, BLOCK:]], axis=1)
        else:
            prob = diagonal
        prob_ref[span, start:] = prob
        dv_low[span] = dot(prob.astype(LOW), g_ref[start:], ((1,), (0,))).astype(LOW)


def score_products(arrays, head, deltas, prob_ref, acc, qk_low, between):
    q_ref, k_ref, g_ref, v_ref = (arrays.at[index, head] for index in range(4))
    tokens, width = q_ref.shape
    scaling = 1.0 / math.sqrt(width)
    for start in range(0, tokens, BLOCK):
        span = slice(start, start + BLOCK)
        dprob = dot(v_ref[span], g_ref[start:], ((1,), (1,)))
        dscore = prob_ref[span, start:] * (dprob - deltas[:, start:]) * scaling
        score_low = dscore.astype(LOW)
        dquery = dot(score_low, k_ref[span], ((0,), (0,)))
        if start == 0:
            acc[...] = dquery
        else:
            acc[start:] += dquery
        qk_low[span, :width] = acc[span].astype(LOW)
        qk_low[span, width:] = dot(score_low, q_ref[start:], ((1,), (0,))).astype(LOW)
        if start == BLOCK:
            between()


def kernel(
    dp_size,
    ctx_size,
    layer_input,
    q_hbm,
    k_hbm,
    v_hbm,
    o_hbm,
    g_hbm,
    layer_grad,
    sums_ref,
    projector,
    out_ref,
    arrays,
    rows_in,
    proj,
    proj_acc,
    grad_own,
    out_own,
    reduced,
    reduced_t,
    reduced_grad,
    delta_out,
    delta_in,
    delta_rows,
    prob_ref,
    acc,
    dv_low,
    qk_low,
    mine_v,
    core_out_v,
    core_in_v,
    core_out_qk,
    core_in_qk,
    total_ref,
    far_out,
    far_in,
    final_own,
    final_out,
    final_in,
    last_own_v,
    last_out_v,
    last_in_v,
    last_own_qk,
    last_out_qk,
    last_in_qk,
    own_o,
    sum_out_o,
    sum_in_o,
    final_own_o,
    final_out_o,
    final_in_o,
    load_sem,
    local_sem,
    head_send,
    head_recv,
    red_send,
    red_recv,
    pass_send,
    pass_recv,
    delta_send,
    delta_recv,
    core_send,
    core_recv,
    far_send,
    far_recv,
    final_send,
    final_recv,
    last_send,
    last_recv,
    sum_send_o,
    sum_recv_o,
    final_send_o,
    final_recv_o,
    known,
):
    me = lax.axis_index("ctx")
    place = lax.axis_index("dp")
    bits = dp_size.bit_length() - 1
    fars = dp_size // 2
    core = lax.rem(place, 2)
    far = place // 2
    sources = (q_hbm, k_hbm, g_hbm, v_hbm)
    count = len(sources)
    heads = arrays.shape[1]
    last = heads - 1
    rows = q_hbm.shape[0]
    width = arrays.shape[3]
    depth = projector.shape[0]
    rank = projector.shape[1]
    piece = rank // dp_size
    slab = piece // ctx_size
    both = 2 * width
    passing = ctx_size == 4
    near = ctx_size == 4 and fars == 4
    mine = pl.ds(pl.multiple_of(me * rows, 16), rows)
    ctx_steps = range(1, ctx_size)

    def columns(owner, head):
        return pl.ds(pl.multiple_of((owner * heads + head) * width, width), width)

    def remote(src, dst, send, recv, **where):
        return pltpu.make_async_remote_copy(
            src_ref=src,
            dst_ref=dst,
            send_sem=send,
            recv_sem=recv,
            device_id=where,
            device_id_type=MESH,
        )

    def local_copy(head, index):
        return pltpu.make_async_copy(
            sources[index].at[:, columns(me, head)],
            arrays.at[index, head, mine],
            local_sem.at[head, index],
        )

    def head_copy(head, index, d):
        peer = me ^ d
        return remote(
            sources[index].at[:, columns(peer, head)],
            arrays.at[index, head, mine],
            head_send.at[head, index, d - 1],
            head_recv.at[head, index, d - 1],
            ctx=peer,
        )

    def start_head(head, indices):
        for index in indices:
            for d in reversed(ctx_steps):
                head_copy(head, index, d).start()
        for index in indices:
            local_copy(head, index).start()

    def wait_sent(head):
        for index in range(count):
            for d in ctx_steps:
                head_copy(head, index, d).wait_send()

    def wait_head(head, indices):
        for index in indices:
            local_copy(head, index).wait()
            for d in ctx_steps:
                head_copy(head, index, d).wait_recv()

    red_steps = (1, 2) if passing else tuple(ctx_steps)

    def reduced_copy(d):
        return remote(
            reduced.at[mine],
            reduced.at[mine],
            red_send.at[d - 1],
            red_recv.at[d - 1],
            ctx=me ^ d,
        )

    def pass_copy(d):
        half = rows // 2
        at = pl.ds(pl.multiple_of((me ^ d) * rows + (d - 1) * half, 16), half)
        return remote(
            reduced.at[at],
            reduced.at[at],
            pass_send.at[d - 1],
            pass_recv.at[d - 1],
            ctx=me ^ (3 - d),
        )

    def delta_copy(d):
        peer = me ^ d
        return remote(
            delta_out.at[peer],
            delta_in.at[me],
            delta_send.at[d - 1],
            delta_recv.at[d - 1],
            ctx=peer,
        )

    def core_copy(head, part):
        out, arrived = ((core_out_v, core_in_v), (core_out_qk, core_in_qk))[part]
        return remote(
            out.at[head],
            arrived.at[head],
            core_send.at[head, part],
            core_recv.at[head, part],
            dp=place ^ 1,
        )

    def far_copy(head, part, d):
        lanes = (pl.ds(both, width), pl.ds(0, both))[part]
        return remote(
            far_out.at[head, far ^ d, :, lanes],
            far_in.at[head, d - 1, :, lanes],
            far_send.at[head, part, d - 1],
            far_recv.at[head, part, d - 1],
            dp=place ^ (2 * d),
        )

    def final_copy(head, d):
        peer = me ^ d
        return remote(
            final_out.at[head, peer],
            final_in.at[head, d - 1],
            final_send.at[head, d - 1],
            final_recv.at[head, d - 1],
            ctx=peer,
        )

    def last_copy(part, f, d):
        out, arrived = ((last_out_v, last_in_v), (last_out_qk, last_in_qk))[part]
        return remote(
            out.at[(far ^ f) * ctx_size + (me ^ d)],
            arrived.at[f * ctx_size + d],
            last_send.at[part],
            last_recv.at[part],
            dp=place ^ (2 * f),
            ctx=me ^ d,
        )

    def wait_last(part):
        arrived = (last_in_v, last_in_qk)[part]
        all_others = arrived.at[pl.ds(1, fars * ctx_size - 1)]
        for sem in (last_recv, last_send):
            pltpu.make_async_copy(all_others, all_others, sem.at[part]).wait()

    last_steps = [
        (f, d) for f in reversed(range(fars)) for d in reversed(range(ctx_size)) if f or d
    ]

    def group_o(chunk):
        return tuple(ref.at[chunk] for ref in (own_o, sum_out_o, sum_in_o, sum_send_o, sum_recv_o))

    def place_bit(stage):
        return lax.rem(place // 2**stage, 2)

    def stage_copy(group, stage):
        half = dp_size // 2 ** (stage + 1)
        span = pl.ds(dp_size - 2 * half, half)
        return remote(
            group[1].at[span],
            group[2].at[span],
            group[3].at[stage],
            group[4].at[stage],
            dp=place ^ 2**stage,
        )

    def stage_blocks(stage, bit):
        half = dp_size // 2 ** (stage + 1)
        first = lax.rem(place, 2**stage) + bit * 2**stage
        return [(first + 2 ** (stage + 1) * j, dp_size - 2 * half + j) for j in range(half)]

    def send_stage(group, stage):
        for block, slot in stage_blocks(stage, 1 - place_bit(stage)):
            group[1][slot] = group[0][block].astype(LOW)
        stage_copy(group, stage).start()

    def add_stage(group, stage):
        stage_copy(group, stage).wait_recv()
        for block, slot in stage_blocks(stage, place_bit(stage)):
            group[0][block] += group[2][slot].astype(WIDE)

    def final_copy_o(chunk, d):
        peer = me ^ d
        return remote(
            final_out_o.at[chunk, peer],
            final_in_o.at[chunk, d - 1],
            final_send_o.at[chunk, d - 1],
            final_recv_o.at[chunk, d - 1],
            ctx=peer,
        )

    def advance_o(chunk, stage):
        group = group_o(chunk)
        add_stage(group, stage)
        if stage + 1 < bits:
            send_stage(group, stage + 1)
            return
        total = own_o[chunk, place]
        for to in range(ctx_size):
            part = total[to * slab : (to + 1) * slab]
            final_own_o[chunk, to] = part
            final_out_o[chunk, to] = part.astype(LOW)
        for d in ctx_steps:
            final_copy_o(chunk, d).start()

    loads = (
        pltpu.make_async_copy(projector, proj, load_sem.at[0]),
        pltpu.make_async_copy(layer_input, rows_in.at[:rows], load_sem.at[1]),
        pltpu.make_async_copy(layer_grad, rows_in.at[rows:], load_sem.at[2]),
        pltpu.make_async_copy(o_hbm, out_own, load_sem.at[3]),
        pltpu.make_async_copy(g_hbm, grad_own, load_sem.at[4]),
    )
    barrier = pltpu.get_barrier_semaphore()
    greet_ctx = (1, 2) if near else tuple(ctx_steps)
    greet_dp = (0,) if near else tuple(range(bits))
    for d in greet_ctx:
        pl.semaphore_signal(barrier, inc=1, device_id={"ctx": me ^ d}, device_id_type=MESH)
    for stage in greet_dp:
        peer = place ^ 2**stage
        pl.semaphore_signal(barrier, inc=1, device_id={"dp": peer}, device_id_type=MESH)
    if near:

        @pl.when(far > 0)
        def _():
            pl.semaphore_signal(barrier, inc=1, device_id={"dp": place - 2}, device_id_type=MESH)

        @pl.when(far < fars - 1)
        def _():
            pl.semaphore_signal(barrier, inc=1, device_id={"dp": place + 2}, device_id_type=MESH)

    for load in loads:
        load.start()
    greeted = len(greet_ctx) + len(greet_dp)
    if near:
        inner = jnp.logical_and(far > 0, far < fars - 1)
        pl.semaphore_wait(barrier, greeted + 1 + inner.astype(jnp.int32))
        for index in range(2):
            for d in (1, 2):
                head_copy(0, index, d).start()
        pl.semaphore_signal(known.at[0], inc=1, device_id={"ctx": me ^ 1}, device_id_type=MESH)

        @pl.when(inner)
        def _():
            for step in (-2, 2):
                pl.semaphore_signal(
                    known.at[1], inc=1, device_id={"dp": place + step}, device_id_type=MESH
                )

        pl.semaphore_wait(known.at[0], 1)
        for index in range(2):
            head_copy(0, index, 3).start()
            local_copy(0, index).start()
    else:
        pl.semaphore_wait(barrier, greeted)
        start_head(0, range(2))
    for load in loads[:3]:
        load.wait()
    proj_acc[...] = jnp.zeros_like(proj_acc)

    @pl.loop(0, depth // DEPTH)
    def _(step):
        at = pl.ds(pl.multiple_of(step * DEPTH, DEPTH), DEPTH)
        proj_acc[...] += dot(rows_in[:, at], proj[at], ((1,), (0,)))

    reduced[mine] = proj_acc[:rows].astype(LOW)
    for d in red_steps:
        reduced_copy(d).start()
    start_head(0, range(2, count))
    reduced_grad[...] = proj_acc[rows:].astype(LOW)
    for load in loads[3:]:
        load.wait()
    rgrad_t = reduced_grad[...].T
    part_width = own_o.shape[3]
    for chunk in range(CHUNKS):
        at = slice(chunk * part_width, (chunk + 1) * part_width)
        for part in range(dp_size):
            span = slice(part * piece, (part + 1) * piece)
            own_o[chunk, part] = dot(rgrad_t[span], out_own[:, at], ((1,), (0,)))
        send_stage(group_o(chunk), 0)

    if near:
        pl.semaphore_wait(known.at[1], 1)
    for chunk in range(2):
        advance_o(chunk, 0)

    def complete_o(chunks):
        for chunk in chunks:
            for stage in range(2, bits):
                advance_o(chunk, stage)

    lane = lax.broadcasted_iota(jnp.int32, (rows, BLOCK), 1)
    table = jnp.zeros((rows, BLOCK), WIDE)
    for head in range(heads * ctx_size):
        span = slice(head * width, (head + 1) * width)
        product = grad_own[:, span].astype(WIDE) * out_own[:, span].astype(WIDE)
        table = jnp.where(lane == head, jnp.sum(product, axis=1, keepdims=True), table)
    table = table.T
    delta_out[...] = jnp.zeros_like(delta_out)
    for owner in range(ctx_size):
        delta_out[owner, :heads] = table[owner * heads : (owner + 1) * heads]
    delta_in[me] = delta_out[me]
    for d in ctx_steps:
        delta_copy(d).start()
    for d in red_steps:
        reduced_copy(d).wait_recv()
        if passing:
            pass_copy(d).start()
    for head in range(1, heads):
        start_head(head, range(count))
    advance_o(2, 0)
    advance_o(0, 1)

    def gather_reduced():
        advance_o(1, 1)
        advance_o(3, 0)
        for d in ctx_steps:
            delta_copy(d).wait_recv()
        delta_rows[...] = jnp.concatenate([delta_in[owner] for owner in range(ctx_size)], axis=1)
        if passing:
            for d in red_steps:
                pass_copy(d).wait_recv()
        turned = reduced[...].T
        for part in range(dp_size):
            block = turned[part * piece : (part + 1) * piece]
            reduced_t[part % 2, (part // 2) * piece : (part // 2 + 1) * piece] = block

    def keep(head, total, lanes):
        for f in range(fars):
            block = total[f * piece : (f + 1) * piece]
            total_ref[head, f, :, lanes] = block
            far_out[head, f, :, lanes] = block.astype(LOW)

    def send_last(total, part):
        own, out = ((last_own_v, last_out_v), (last_own_qk, last_out_qk))[part]
        for f in range(fars):
            for to in range(ctx_size):
                first = f * piece + to * slab
                block = total[first : first + slab]
                own[f, to] = block
                out[f * ctx_size + to] = block.astype(LOW)
        for f, d in last_steps:
            last_copy(part, f, d).start()

    def finish(head):
        total = total_ref[head, far]
        for d in range(1, fars):
            for part in range(2):
                far_copy(head, part, d).wait_recv()
            total += far_in[head, d - 1].astype(WIDE)
        for to in range(ctx_size):
            block = total[to * slab : (to + 1) * slab]
            final_own[head, to] = block
            final_out[head, to] = block.astype(LOW)
        for d in ctx_steps:
            final_copy(head, d).start()

    @pl.loop(0, heads)
    def _(head):
        wait_head(head, range(3))
        sums = sums_ref[pl.ds(me * heads + head, 1), :]
        value_products(arrays, head, sums, prob_ref, dv_low)

        @pl.when(head == 0)
        def _():
            gather_reduced()

        @pl.when(head == 1)
        def _():
            advance_o(3, 1)

        low = dv_low[...]
        core_out_v[head] = dot(reduced_t[1 - core], low, ((1,), (0,))).astype(LOW)
        core_copy(head, 0).start()
        mine_v[...] = dot(reduced_t[core], low, ((1,), (0,)))

        def add_values():
            core_copy(head, 0).wait_recv()
            total = mine_v[...] + core_in_v[head].astype(WIDE)

            @pl.when(head < last)
            def _():
                keep(head, total, slice(both, both + width))
                for d in reversed(range(1, fars)):
                    far_copy(head, 0, d).start()

            @pl.when(head == last)
            def _():
                send_last(total, 0)

        wait_head(head, range(3, count))
        deltas = delta_rows[pl.ds(head, 1), :]
        score_products(arrays, head, deltas, prob_ref, acc, qk_low, add_values)
        low = qk_low[...]
        core_out_qk[head] = dot(reduced_t[1 - core], low, ((1,), (0,))).astype(LOW)
        core_copy(head, 1).start()
        joined = dot(reduced_t[core], low, ((1,), (0,)))
        core_copy(head, 1).wait_recv()
        total = joined + core_in_qk[head].astype(WIDE)

        @pl.when(head < last)
        def _():
            keep(head, total, slice(0, both))
            for d in reversed(range(1, fars)):
                far_copy(head, 1, d).start()

        @pl.when(head == last)
        def _():
            send_last(total, 1)

        @pl.when(head == 0)
        def _():
            advance_o(2, 1)

        @pl.when(head == max(last - 1, 1))
        def _():
            complete_o(range(CHUNKS))

        @pl.when(head < last)
        def _():
            for part in range(2):
                core_copy(head, part).wait_send()
            wait_sent(head)

    for d in red_steps:
        reduced_copy(d).wait_send()
    if passing:
        for d in red_steps:
            pass_copy(d).wait_send()
    for d in ctx_steps:
        delta_copy(d).wait_send()
    for chunk in range(CHUNKS):
        for stage in range(bits):
            stage_copy(group_o(chunk), stage).wait_send()
    for head in range(last):
        finish(head)
    for part in range(2):
        core_copy(last, part).wait_send()
    wait_sent(last)

    for chunk in range(CHUNKS):
        at = slice(chunk * part_width, (chunk + 1) * part_width)
        total = final_own_o[chunk, me]
        for d in ctx_steps:
            final_copy_o(chunk, d).wait()
            total += final_in_o[chunk, d - 1].astype(WIDE)
        out_ref[3, :, at] = total

    for head in range(last):
        for d in range(1, fars):
            for part in range(2):
                far_copy(head, part, d).wait_send()
        for d in range(ctx_size):
            if d:
                final_copy(head, d).wait()
                block = final_in[head, d - 1].astype(WIDE)
            else:
                block = final_own[head, me]
            for index in range(3):
                span = slice(index * width, (index + 1) * width)
                out_ref[index, :, columns(me ^ d, head)] = block[:, span]

    for part, own, arrived, first in ((0, last_own_v, last_in_v, 2), (1, last_own_qk, last_in_qk, 0)):
        wait_last(part)
        for d in range(ctx_size):
            total = None if d else own[far, me]
            for f in range(fars):
                if f or d:
                    block = arrived[f * ctx_size + d].astype(WIDE)
                    total = block if total is None else total + block
            for index in range(own.shape[3] // width):
                span = slice(index * width, (index + 1) * width)
                out_ref[first + index, :, columns(me ^ d, last)] = total[:, span]


def on_device(
    dp_size,
    ctx_size,
    layer_input,
    queries,
    key_rows,
    value_rows,
    attn_out,
    out_grad,
    layer_grad,
    logsum,
    projector,
):
    rows, features = queries.shape[1:]
    all_heads, tokens = logsum.shape[1:]
    heads = all_heads // ctx_size
    width = features // all_heads
    depth, rank = projector.shape
    bits = dp_size.bit_length() - 1
    fars = dp_size // 2
    piece = rank // dp_size
    slab = piece // ctx_size
    padded = -(-heads // 8) * 8
    half = rank // 2
    both = 2 * width
    three = 3 * width
    part_width = features // CHUNKS
    others = ctx_size - 1
    dma = pltpu.SemaphoreType.DMA
    anywhere = pl.BlockSpec(memory_space=pl.ANY)
    in_vmem = pl.BlockSpec(memory_space=pltpu.VMEM)
    return pl.pallas_call(
        functools.partial(kernel, dp_size, ctx_size),
        out_shape=pltpu.VMEM((4, slab, features), WIDE),
        in_specs=[anywhere] * 7 + [in_vmem, anywhere],
        out_specs=in_vmem,
        scratch_shapes=[
            pltpu.VMEM((4, heads, tokens, width), LOW),
            pltpu.VMEM((2 * rows, depth), LOW),
            pltpu.VMEM((depth, rank), LOW),
            pltpu.VMEM((2 * rows, rank), WIDE),
            pltpu.VMEM((rows, features), LOW),
            pltpu.VMEM((rows, features), LOW),
            pltpu.VMEM((tokens, rank), LOW),
            pltpu.VMEM((2, half, tokens), LOW),
            pltpu.VMEM((rows, rank), LOW),
            pltpu.VMEM((ctx_size, padded, rows), WIDE),
            pltpu.VMEM((ctx_size, padded, rows), WIDE),
            pltpu.VMEM((padded, tokens), WIDE),
            pltpu.VMEM((tokens, tokens), WIDE),
            pltpu.VMEM((tokens, width), WIDE),
            pltpu.VMEM((tokens, width), LOW),
            pltpu.VMEM((tokens, both), LOW),
            pltpu.VMEM((half, width), WIDE),
            pltpu.VMEM((heads, half, width), LOW),
            pltpu.VMEM((heads, half, width), LOW),
            pltpu.VMEM((heads, half, both), LOW),
            pltpu.VMEM((heads, half, both), LOW),
            pltpu.VMEM((heads, fars, piece, three), WIDE),
            pltpu.VMEM((heads, fars, piece, three), LOW),
            pltpu.VMEM((heads, fars - 1, piece, three), LOW),
            pltpu.VMEM((heads, ctx_size, slab, three), WIDE),
            pltpu.VMEM((heads, ctx_size, slab, three), LOW),
            pltpu.VMEM((heads, others, slab, three), LOW),
            pltpu.VMEM((fars, ctx_size, slab, width), WIDE),
            pltpu.VMEM((fars * ctx_size, slab, width), LOW),
            pltpu.VMEM((fars * ctx_size, slab, width), LOW),
            pltpu.VMEM((fars, ctx_size, slab, both), WIDE),
            pltpu.VMEM((fars * ctx_size, slab, both), LOW),
            pltpu.VMEM((fars * ctx_size, slab, both), LOW),
            pltpu.VMEM((CHUNKS, dp_size, piece, part_width), WIDE),
            pltpu.VMEM((CHUNKS, dp_size - 1, piece, part_width), LOW),
            pltpu.VMEM((CHUNKS, dp_size - 1, piece, part_width), LOW),
            pltpu.VMEM((CHUNKS, ctx_size, slab, part_width), WIDE),
            pltpu.VMEM((CHUNKS, ctx_size, slab, part_width), LOW),
            pltpu.VMEM((CHUNKS, others, slab, part_width), LOW),
            dma((5,)),
            dma((heads, 4)),
            dma((heads, 4, others)),
            dma((heads, 4, others)),
            dma((others,)),
            dma((others,)),
            dma((2,)),
            dma((2,)),
            dma((others,)),
            dma((others,)),
            dma((heads, 2)),
            dma((heads, 2)),
            dma((heads, 2, fars - 1)),
            dma((heads, 2, fars - 1)),
            dma((heads, others)),
            dma((heads, others)),
            dma((2,)),
            dma((2,)),
            dma((CHUNKS, bits)),
            dma((CHUNKS, bits)),
            dma((CHUNKS, others)),
            dma((CHUNKS, others)),
            pltpu.SemaphoreType.REGULAR((2,)),
        ],
        compiler_params=pltpu.CompilerParams(
            collective_id=0, has_side_effects=True, vmem_limit_bytes=56 * 1024 * 1024
        ),
    )(
        layer_input[0],
        queries[0],
        key_rows[0],
        value_rows[0],
        attn_out[0],
        out_grad[0],
        layer_grad[0],
        logsum[0],
        projector,
    )


def solution(mesh):
    rows = P("dp", "ctx", None)
    placed = (rows,) * 7 + (P("dp", None, None), P())
    return jax.shard_map(
        functools.partial(on_device, mesh.shape["dp"], mesh.shape["ctx"]),
        mesh=mesh,
        in_specs=placed,
        out_specs=P(None, ("dp", "ctx"), None),
        check_vma=False,
    )
```
